32 devices in a mesh: dp: 8 (over y, x, core), seq: 4 (over z).
Axes of the slice: x: 2, y: 2, z: 4, core: 2. Of those that a mesh axis runs over, the one named last changes fastest.
Arguments:
- tokens_in: bfloat16 [16, 580, 1024], P('dp', 'seq'), may hold values from -6 to 6
- cotangent: bfloat16 [16, 580, 1024], P('dp', 'seq'), may hold values from -6 to 6
- group_count: int32 [8], P('dp'), may hold values from 1 to 2, as said below
- key_mask: int32 [16, 580], P('dp'), may hold values from 0 to 1, as said below
- ln1_gain: float32 [1024], P(('dp', 'seq')), may hold values from 0.5 to 1.5
- ln1_shift: float32 [1024], P(('dp', 'seq')), may hold values from -3 to 3
- w_query: float32 [1024, 1024], P(('dp', 'seq')), may hold values from -0.25 to 0.25
- b_query: float32 [1024], P(('dp', 'seq')), may hold values from -3 to 3
- w_key: float32 [1024, 1024], P(('dp', 'seq')), may hold values from -0.1875 to 0.1875
- w_value: float32 [1024, 1024], P(('dp', 'seq')), may hold values from -0.1875 to 0.1875
- b_value: float32 [1024], P(('dp', 'seq')), may hold values from -0.6 to 0.6
- w_out: float32 [1024, 1024], P(('dp', 'seq')), may hold values from -1.5 to 1.5
- b_out: float32 [1024], P(('dp', 'seq')), may hold values from -3 to 3
- ln2_gain: float32 [1024], P(('dp', 'seq')), may hold values from 0.5 to 1.5
- ln2_shift: float32 [1024], P(('dp', 'seq')), may hold values from -3 to 3
- w_up: float32 [1024, 4096], P(('dp', 'seq')), may hold values from -0.1875 to 0.1875
- b_up: float32 [4096], P(('dp', 'seq')), may hold values from -3 to 3
- w_down: float32 [4096, 1024], P(('dp', 'seq')), may hold values from -0.09375 to 0.09375
- b_down: float32 [1024], P(('dp', 'seq')), may hold values from -3 to 3
Outputs:
- block_out: bfloat16 [16, 580, 1024], P('dp', 'seq')
- input_grad: bfloat16 [16, 580, 1024], P('dp', 'seq')
- grad_ln1_gain: float32 [1024], P(('dp', 'seq'))
- grad_ln1_shift: float32 [1024], P(('dp', 'seq'))
- grad_w_query: float32 [1024, 1024], P(('dp', 'seq'))
- grad_b_query: float32 [1024], P(('dp', 'seq'))
- grad_w_key: float32 [1024, 1024], P(('dp', 'seq'))
- grad_w_value: float32 [1024, 1024], P(('dp', 'seq'))
- grad_b_value: float32 [1024], P(('dp', 'seq'))
- grad_w_out: float32 [1024, 1024], P(('dp', 'seq'))
- grad_b_out: float32 [1024], P(('dp', 'seq'))
- grad_ln2_gain: float32 [1024], P(('dp', 'seq'))
- grad_ln2_shift: float32 [1024], P(('dp', 'seq'))
- grad_w_up: float32 [1024, 4096], P(('dp', 'seq'))
- grad_b_up: float32 [4096], P(('dp', 'seq'))
- grad_w_down: float32 [4096, 1024], P(('dp', 'seq'))
- grad_b_down: float32 [1024], P(('dp', 'seq'))
The draws below stay inside these ranges and needn't reach their ends.
Inputs may be any that keep to these rules, and one draw needn't show every extreme that they name: A data group's images fill its first group_count slots; some group holds 2. `key_mask`: the first token of every image is a key; positions 577 and later never are.
All inputs are finite; a program needn't handle non-finite values.
Results may differ from the reference program's by a relative error of at most 0.013.
The reference program's roundings to bfloat16 on the way count: a program that leaves them out, or rounds other values in their place, can miss the bound.
Values may be sent and summed in bfloat16 or wider, within the bound.
No kernel may reach another device: no remote copies, remote signals or barrier semaphores. Data moves between devices by JAX's collectives and lax.ppermute only.
A program may use at most 192 MiB of HBM per device.

```python
from functools import partial
import jax
import jax.numpy as jnp
from jax import lax

D = 1024
HEADS = 16
HD = 64
FF = 4096
IMG_TOK = 577
SLOTS = 2
IMAGES = 16
LP = 580
N_DP = 8


def draw_group_count(key, part):
    lowest = max(1, SLOTS // 4)
    counts = jax.random.randint(key, (N_DP,), lowest, SLOTS + 1)
    fullest = jax.random.randint(jax.random.fold_in(key, 7), (), 0, N_DP)
    return jnp.where(jnp.arange(N_DP) == fullest, SLOTS, counts).astype(jnp.int32)


def draw_key_mask(key, part):
    quarter = jax.random.randint(jax.random.fold_in(key, 11), (IMAGES, LP), 0, 4)
    position = jnp.arange(LP)[None, :]
    chosen = jnp.where(position == 0, 1, (quarter > 0).astype(jnp.int32))
    return jnp.where(position < IMG_TOK, chosen, 0).astype(jnp.int32)


def level_of(rng, dims, cuts, smallest, high):
    factor_of, own = 1.0, jax.random.fold_in(rng, 6)
    for dim, parts in cuts:
        heights = jnp.exp(jax.random.uniform(jax.random.fold_in(own, dim), (parts,), jnp.float32, smallest / len(cuts), high / len(cuts)))
        factor_of = factor_of * jnp.repeat(heights, dims[dim] // parts).reshape([-1 if axis == dim else 1 for axis in range(len(dims))])
    return factor_of


def noise(key, extent, width, reach, split=(), kind=jnp.bfloat16):
    result = width * jax.random.normal(key, extent, jnp.float32)
    if split:
        result = result * level_of(key, extent, split, -0.22, 0.18)
    return jnp.clip(result, -reach, reach).astype(kind)


def setup_inputs(seed: int = 0) -> dict:
    key_of = jax.random.split(jax.random.key(seed), 20)
    return {
        "tokens_in": noise(key_of[0], (IMAGES, LP, D), 1.0, 6.0, ((0, 8), (1, 4))),
        "cotangent": noise(key_of[1], (IMAGES, LP, D), 1.0, 6.0, ((0, 8), (1, 4))),
        "group_count": draw_group_count(jax.random.fold_in(key_of[19], 71), 0),
        "key_mask": draw_key_mask(jax.random.fold_in(key_of[19], 71), 0),
        "ln1_gain": jnp.clip(1.0 + 0.1 * jax.random.normal(key_of[4], (D,), jnp.float32), 0.5, 1.5),
        "ln1_shift": noise(key_of[5], (D,), 0.5, 3.0, ((0, 32),), jnp.float32),
        "w_query": noise(key_of[6], (D, D), (D // 2) ** -0.5, 0.25, ((0, 32),), jnp.float32),
        "b_query": noise(key_of[7], (D,), 0.5, 3.0, ((0, 32),), jnp.float32),
        "w_key": noise(key_of[8], (D, D), D ** -0.5, 0.1875, ((0, 32),), jnp.float32),
        "w_value": noise(key_of[9], (D, D), D ** -0.5, 0.1875, ((0, 32),), jnp.float32),
        "b_value": noise(key_of[10], (D,), 0.1, 0.6, ((0, 32),), jnp.float32),
        "w_out": noise(key_of[11], (D, D), 16 ** -0.5, 1.5, ((0, 32),), jnp.float32),
        "b_out": noise(key_of[12], (D,), 0.5, 3.0, ((0, 32),), jnp.float32),
        "ln2_gain": jnp.clip(1.0 + 0.1 * jax.random.normal(key_of[13], (D,), jnp.float32), 0.5, 1.5),
        "ln2_shift": noise(key_of[14], (D,), 0.5, 3.0, ((0, 32),), jnp.float32),
        "w_up": noise(key_of[15], (D, FF), D ** -0.5, 0.1875, ((0, 32),), jnp.float32),
        "b_up": noise(key_of[16], (FF,), 0.5, 3.0, ((0, 32),), jnp.float32),
        "w_down": noise(key_of[17], (FF, D), FF ** -0.5, 0.09375, ((0, 32),), jnp.float32),
        "b_down": noise(key_of[18], (D,), 0.5, 3.0, ((0, 32),), jnp.float32),
    }


@jax.custom_vjp
def low(v):
    return lax.optimization_barrier(v.astype(jnp.bfloat16)).astype(jnp.float32)

@jax.custom_vjp
def low_back(v):
    return v

def low_keep(v):
    return (low(v), None)

def low_pass(kept, grad):
    return (grad,)

def back_keep(v):
    return (v, None)

def back_low(kept, grad):
    return (low(grad),)
low.defvjp(low_keep, low_pass)
low_back.defvjp(back_keep, back_low)
EPSILON = 1e-05
SLOPE = 1.702
MASKED = -1000000000.0

def matmul(left, right):
    return jnp.dot(left, right, precision=lax.Precision.HIGHEST, preferred_element_type=jnp.float32)

def layer_norm(values, gain, shift):
    center = values - lax.optimization_barrier(jnp.mean(values, axis=-1, keepdims=True))
    spread = lax.optimization_barrier(jnp.mean(center * center, axis=-1, keepdims=True))
    return center * lax.rsqrt(spread + EPSILON) * gain + shift

def one_image(params, image, key_keep):
    gain_one, shift_one, query_w, query_b, key_w, value_w, value_b, out_w, out_b, gain_two, shift_two, up_w, up_b, down_w, down_b = params
    normed_one = low(layer_norm(image, gain_one, shift_one))
    queries = low_back(low(matmul(normed_one, query_w) + query_b)).reshape(LP, HEADS, HD)
    keys_all = low_back(low(matmul(normed_one, key_w))).reshape(LP, HEADS, HD)
    values_all = low_back(low(matmul(normed_one, value_w) + value_b)).reshape(LP, HEADS, HD)
    scores = jnp.einsum('qhd,khd->hqk', queries, keys_all, precision=lax.Precision.HIGHEST) * HD ** (-0.5)
    scores = low_back(jnp.where(key_keep[None, None, :] > 0, scores, MASKED))
    row_peak = lax.optimization_barrier(jnp.max(scores, axis=-1, keepdims=True))
    weights_exp = jnp.exp(scores - row_peak)
    weights_soft = weights_exp / lax.optimization_barrier(jnp.sum(weights_exp, axis=-1, keepdims=True))
    mixed_out = jnp.einsum('hqk,khd->qhd', low(weights_soft), values_all, precision=lax.Precision.HIGHEST)
    mixed_out = low_back(low(mixed_out.reshape(LP, D)))
    branch = low_back(matmul(mixed_out, out_w) + out_b)
    middle = image + branch
    normed_two = low(layer_norm(middle, gain_two, shift_two))
    hidden = low_back(matmul(normed_two, up_w) + up_b)
    activated = low(hidden * jax.nn.sigmoid(SLOPE * hidden))
    return middle + matmul(activated, down_w) + down_b

def reference(tokens_in, cotangent, group_count, key_mask, ln1_gain, ln1_shift, w_query, b_query, w_key, w_value, b_value, w_out, b_out, ln2_gain, ln2_shift, w_up, b_up, w_down, b_down):
    masters = (ln1_gain, ln1_shift, w_query, b_query, w_key, w_value, b_value, w_out, b_out, ln2_gain, ln2_shift, w_up, b_up, w_down, b_down)
    slot_place = jnp.arange(IMAGES, dtype=jnp.int32) % SLOTS
    live = (slot_place < jnp.repeat(group_count, SLOTS)).astype(jnp.float32)
    images = tokens_in.astype(jnp.float32)

    def forward(params, inputs):
        rounded = tuple((low(master) for master in params))
        step_fn = jax.checkpoint(partial(one_image, rounded))
        return lax.map(lambda paired: step_fn(paired[0], paired[1]), (inputs, key_mask))
    outputs, pullback = jax.vjp(forward, masters, images)
    live_rows = live[:, None, None]
    grads, grad_images = pullback(cotangent.astype(jnp.float32) * live_rows)
    block_out = (outputs * live_rows).astype(jnp.bfloat16)
    return (block_out, grad_images.astype(jnp.bfloat16), grads[0], grads[1], grads[2], grads[3], grads[4], grads[5], grads[6], grads[7], grads[8], grads[9], grads[10], grads[11], grads[12], grads[13], grads[14])
```

```python
import jax
import jax.numpy as jnp
from jax import lax
from jax.sharding import PartitionSpec as P

HD = 64


EPSILON = 1e-05
SLOPE = 1.702
MASKED = -1000000000.0


def norm_stats(values):
    center = values - jnp.mean(values, axis=-1, keepdims=True)
    inverse = lax.rsqrt(jnp.mean(center * center, axis=-1, keepdims=True) + EPSILON)
    return (center * inverse, inverse)


def norm_back(incoming, normal, inverse, gain):
    scaled = incoming * gain
    rows_grad = inverse * (
        scaled
        - jnp.mean(scaled, axis=-1, keepdims=True)
        - normal * jnp.mean(scaled * normal, axis=-1, keepdims=True)
    )
    return (rows_grad, jnp.sum(incoming * normal, axis=0), jnp.sum(incoming, axis=0))


def product(left, right):
    return jnp.dot(left, right, preferred_element_type=jnp.float32)


def contract_rows(left, right):
    return lax.dot_general(
        left, right, (((0,), (0,)), ((), ())), preferred_element_type=jnp.float32
    )


def contract_cols(left, right):
    return lax.dot_general(
        left, right, (((1,), (1,)), ((), ())), preferred_element_type=jnp.float32
    )


def split_heads(stacked):
    length = stacked.shape[0]
    heads_here = stacked.shape[2] // HD
    queries = stacked[:, 0].reshape(length, heads_here, HD)
    keys_all = stacked[:, 1].reshape(length, heads_here, HD)
    values_all = stacked[:, 2].reshape(length, heads_here, HD)
    return (queries, keys_all, values_all)


def masked_scores(queries, keys_all, key_keep):
    scores = jnp.einsum(
        "qhd,khd->hqk", queries, keys_all, preferred_element_type=jnp.float32
    ) * HD ** (-0.5)
    return jnp.where(key_keep[None, None, :] > 0, scores, MASKED)


def attend_image(paired):
    stacked, key_keep = paired
    queries, keys_all, values_all = split_heads(stacked)
    scores = masked_scores(queries, keys_all, key_keep)
    row_peak = jnp.max(scores, axis=-1, keepdims=True)
    weights_exp = jnp.exp(scores - row_peak)
    row_total = jnp.sum(weights_exp, axis=-1, keepdims=True)
    weights_soft = weights_exp / row_total
    mixed_out = jnp.einsum(
        "hqk,khd->qhd",
        weights_soft.astype(jnp.bfloat16),
        values_all,
        preferred_element_type=jnp.float32,
    )
    log_total = (row_peak + jnp.log(row_total))[..., 0]
    return (mixed_out.reshape(stacked.shape[0], stacked.shape[2]).astype(jnp.bfloat16), log_total)


def attend_back(packed):
    stacked, grad_mixed, log_total, key_keep = packed
    queries, keys_all, values_all = split_heads(stacked)
    scores = masked_scores(queries, keys_all, key_keep)
    weights_soft = jnp.exp(scores - log_total[..., None])
    grad_mix = grad_mixed.reshape(queries.shape)
    grad_values = jnp.einsum(
        "hqk,qhd->khd",
        weights_soft.astype(jnp.bfloat16),
        grad_mix,
        preferred_element_type=jnp.float32,
    )
    grad_weights = jnp.einsum(
        "qhd,khd->hqk", grad_mix, values_all, preferred_element_type=jnp.float32
    )
    row_inner = jnp.sum(grad_weights * weights_soft, axis=-1, keepdims=True)
    grad_scores = (weights_soft * (grad_weights - row_inner)).astype(jnp.bfloat16)
    grad_queries = jnp.einsum(
        "hqk,khd->qhd", grad_scores, keys_all, preferred_element_type=jnp.float32
    ) * HD ** (-0.5)
    grad_keys = jnp.einsum(
        "hqk,qhd->khd", grad_scores, queries, preferred_element_type=jnp.float32
    ) * HD ** (-0.5)
    length = stacked.shape[0]
    return jnp.stack(
        [
            grad_queries.reshape(length, -1),
            grad_keys.reshape(length, -1),
            grad_values.reshape(length, -1),
        ],
        axis=1,
    ).astype(jnp.bfloat16)


def per_device(
    tokens_in,
    cotangent,
    group_count,
    key_mask,
    ln1_gain,
    ln1_shift,
    w_query,
    b_query,
    w_key,
    w_value,
    b_value,
    w_out,
    b_out,
    ln2_gain,
    ln2_shift,
    w_up,
    b_up,
    w_down,
    b_down,
):
    slot_count, tok_dev, width = tokens_in.shape
    row_count = slot_count * tok_dev
    shared = (
        lax.all_gather(ln1_gain.astype(jnp.bfloat16), ("dp", "seq"), axis=0, tiled=True),
        lax.all_gather(ln1_shift.astype(jnp.bfloat16), ("dp", "seq"), axis=0, tiled=True),
        lax.all_gather(w_query.astype(jnp.bfloat16), ("dp", "seq"), axis=0, tiled=True),
        lax.all_gather(b_query.astype(jnp.bfloat16), ("dp", "seq"), axis=0, tiled=True),
        lax.all_gather(w_key.astype(jnp.bfloat16), ("dp", "seq"), axis=0, tiled=True),
        lax.all_gather(w_value.astype(jnp.bfloat16), ("dp", "seq"), axis=0, tiled=True),
        lax.all_gather(b_value.astype(jnp.bfloat16), ("dp", "seq"), axis=0, tiled=True),
        lax.all_gather(w_out.astype(jnp.bfloat16), ("dp", "seq"), axis=0, tiled=True),
        lax.all_gather(b_out.astype(jnp.bfloat16), ("dp", "seq"), axis=0, tiled=True),
        lax.all_gather(ln2_gain.astype(jnp.bfloat16), ("dp", "seq"), axis=0, tiled=True),
        lax.all_gather(ln2_shift.astype(jnp.bfloat16), ("dp", "seq"), axis=0, tiled=True),
        lax.all_gather(w_up.astype(jnp.bfloat16), ("dp", "seq"), axis=0, tiled=True),
        lax.all_gather(b_up.astype(jnp.bfloat16), ("dp", "seq"), axis=0, tiled=True),
        lax.all_gather(w_down.astype(jnp.bfloat16), ("dp", "seq"), axis=0, tiled=True),
        lax.all_gather(b_down.astype(jnp.bfloat16), ("dp", "seq"), axis=0, tiled=True),
    )
    (
        gain_one,
        shift_one,
        query_w,
        query_b,
        key_w,
        value_w,
        value_b,
        out_w,
        out_b,
        gain_two,
        shift_two,
        up_w,
        up_b,
        down_w,
        down_b,
    ) = shared
    live_slot = (jnp.arange(slot_count) < group_count[0]).astype(jnp.float32)[:, None, None]
    inputs = tokens_in.astype(jnp.float32).reshape(row_count, width)
    normal_one, inverse_one = norm_stats(inputs)
    normed_one = (normal_one * gain_one + shift_one).astype(jnp.bfloat16)
    queries = (product(normed_one, query_w) + query_b).astype(jnp.bfloat16)
    keys_all = product(normed_one, key_w).astype(jnp.bfloat16)
    values_all = (product(normed_one, value_w) + value_b).astype(jnp.bfloat16)
    stacked = jnp.stack([queries, keys_all, values_all], axis=1).reshape(
        slot_count, tok_dev, 3, width
    )
    by_heads = lax.all_to_all(stacked, "seq", split_axis=3, concat_axis=1, tiled=True)
    mixed_heads, log_total = lax.map(attend_image, (by_heads, key_mask))
    mixed_tok = lax.all_to_all(mixed_heads, "seq", split_axis=1, concat_axis=2, tiled=True).reshape(
        row_count, width
    )
    middle = inputs + product(mixed_tok, out_w) + out_b
    normal_two, inverse_two = norm_stats(middle)
    normed_two = (normal_two * gain_two + shift_two).astype(jnp.bfloat16)
    hidden = product(normed_two, up_w) + up_b
    gate_sig = jax.nn.sigmoid(SLOPE * hidden)
    activated = (hidden * gate_sig).astype(jnp.bfloat16)
    result = middle + product(activated, down_w) + down_b
    block_out = (result.reshape(slot_count, tok_dev, width) * live_slot).astype(jnp.bfloat16)
    upstream = (cotangent.astype(jnp.float32) * live_slot).reshape(row_count, width)
    upstream_low = upstream.astype(jnp.bfloat16)
    grad_down = contract_rows(activated, upstream_low)
    grad_down_b = jnp.sum(upstream, axis=0)
    grad_act = contract_cols(upstream_low, down_w)
    grad_hidden = (grad_act * (gate_sig + SLOPE * hidden * gate_sig * (1.0 - gate_sig))).astype(
        jnp.bfloat16
    )
    grad_up = contract_rows(normed_two, grad_hidden)
    grad_up_b = jnp.sum(grad_hidden.astype(jnp.float32), axis=0)
    grad_normed_two = contract_cols(grad_hidden, up_w)
    grad_mid, grad_gain_two, grad_shift_two = norm_back(
        grad_normed_two, normal_two, inverse_two, gain_two
    )
    grad_middle = upstream + grad_mid
    branch_low = grad_middle.astype(jnp.bfloat16)
    grad_out = contract_rows(mixed_tok, branch_low)
    grad_out_b = jnp.sum(branch_low.astype(jnp.float32), axis=0)
    grad_mixed = (
        contract_cols(branch_low, out_w).astype(jnp.bfloat16).reshape(slot_count, tok_dev, width)
    )
    grad_by_heads = lax.all_to_all(grad_mixed, "seq", split_axis=2, concat_axis=1, tiled=True)
    grad_stacked = lax.map(attend_back, (by_heads, grad_by_heads, log_total, key_mask))
    grad_tok = lax.all_to_all(grad_stacked, "seq", split_axis=1, concat_axis=3, tiled=True).reshape(
        row_count, 3, width
    )
    grad_q_rows = grad_tok[:, 0]
    grad_k_rows = grad_tok[:, 1]
    grad_v_rows = grad_tok[:, 2]
    grad_query = contract_rows(normed_one, grad_q_rows)
    grad_query_b = jnp.sum(grad_q_rows.astype(jnp.float32), axis=0)
    grad_key = contract_rows(normed_one, grad_k_rows)
    grad_value = contract_rows(normed_one, grad_v_rows)
    grad_value_b = jnp.sum(grad_v_rows.astype(jnp.float32), axis=0)
    grad_normed_one = (
        contract_cols(grad_q_rows, query_w)
        + contract_cols(grad_k_rows, key_w)
        + contract_cols(grad_v_rows, value_w)
    )
    grad_first, grad_gain_one, grad_shift_one = norm_back(
        grad_normed_one, normal_one, inverse_one, gain_one
    )
    input_grad = (grad_middle + grad_first).astype(jnp.bfloat16).reshape(slot_count, tok_dev, width)
    every_shard = (
        lax.psum_scatter(grad_gain_one, ("dp", "seq"), scatter_dimension=0, tiled=True),
        lax.psum_scatter(grad_shift_one, ("dp", "seq"), scatter_dimension=0, tiled=True),
        lax.psum_scatter(grad_query, ("dp", "seq"), scatter_dimension=0, tiled=True),
        lax.psum_scatter(grad_query_b, ("dp", "seq"), scatter_dimension=0, tiled=True),
        lax.psum_scatter(grad_key, ("dp", "seq"), scatter_dimension=0, tiled=True),
        lax.psum_scatter(grad_value, ("dp", "seq"), scatter_dimension=0, tiled=True),
        lax.psum_scatter(grad_value_b, ("dp", "seq"), scatter_dimension=0, tiled=True),
        lax.psum_scatter(grad_out, ("dp", "seq"), scatter_dimension=0, tiled=True),
        lax.psum_scatter(grad_out_b, ("dp", "seq"), scatter_dimension=0, tiled=True),
        lax.psum_scatter(grad_gain_two, ("dp", "seq"), scatter_dimension=0, tiled=True),
        lax.psum_scatter(grad_shift_two, ("dp", "seq"), scatter_dimension=0, tiled=True),
        lax.psum_scatter(grad_up, ("dp", "seq"), scatter_dimension=0, tiled=True),
        lax.psum_scatter(grad_up_b, ("dp", "seq"), scatter_dimension=0, tiled=True),
        lax.psum_scatter(grad_down, ("dp", "seq"), scatter_dimension=0, tiled=True),
        lax.psum_scatter(grad_down_b, ("dp", "seq"), scatter_dimension=0, tiled=True),
    )
    return (block_out, input_grad) + tuple(every_shard)


def swap_core(value):
    return lax.ppermute(value, "core", [(0, 1), (1, 0)])


def swap_x(value):
    return lax.ppermute(value, "x", [(0, 1), (1, 0)])


def swap_y(value):
    return lax.ppermute(value, "y", [(0, 1), (1, 0)])


def trade_z(value):
    return lax.all_to_all(value, "z", split_axis=0, concat_axis=0, tiled=True)


def in_order(index, mine, other, axis):
    return jnp.where(
        index == 0, jnp.stack([mine, other], axis=axis), jnp.stack([other, mine], axis=axis)
    )


def take(index, value, axis):
    return lax.dynamic_index_in_dim(value, index, axis, keepdims=False)


def gather_z(shard):
    copies = lax.axis_size("z")
    return trade_z(jnp.broadcast_to(shard[None], (copies,) + shard.shape))


def gather_plane(rows):
    here_x, here_y = (lax.axis_index("x"), lax.axis_index("y"))
    half = rows.shape[0] // 2
    first, second = (rows[:half], rows[half:])
    first_x = swap_x(first)
    second_y = swap_y(second)
    first_pair = in_order(here_x, first, first_x, 0)
    second_pair = in_order(here_y, second, second_y, 0)
    first_y = swap_y(first_pair)
    second_x = swap_x(second_pair)
    first_all = in_order(here_y, first_pair, first_y, 0)
    second_all = in_order(here_x, second_pair, second_x, 1)
    return jnp.stack([first_all, second_all], axis=2).reshape(4 * rows.shape[0], rows.shape[1])


def scatter_plane(total):
    here_x, here_y = (lax.axis_index("x"), lax.axis_index("y"))
    rows = total.shape[0] // 4
    half = rows // 2
    blocks = total.reshape(2, 2, 2, half, total.shape[1])
    first, second = (blocks[:, :, 0], blocks[:, :, 1])
    first_got = swap_y(take(1 - here_y, first, 0).astype(jnp.bfloat16))
    second_got = swap_x(take(1 - here_x, second, 1).astype(jnp.bfloat16))
    first_sum = take(here_y, first, 0) + first_got
    second_sum = take(here_x, second, 1) + second_got
    first_last = swap_x(take(1 - here_x, first_sum, 0).astype(jnp.bfloat16))
    second_last = swap_y(take(1 - here_y, second_sum, 0).astype(jnp.bfloat16))
    return jnp.concatenate(
        [
            take(here_x, first_sum, 0) + first_last,
            take(here_y, second_sum, 0) + second_last,
        ],
        axis=0,
    )


def scatter_z(parts):
    return jnp.sum(trade_z(parts.astype(jnp.bfloat16)).astype(jnp.float32), axis=0)


def own_image(
    tokens_in,
    cotangent,
    group_count,
    key_mask,
    ln1_gain,
    ln1_shift,
    w_query,
    b_query,
    w_key,
    w_value,
    b_value,
    w_out,
    b_out,
    ln2_gain,
    ln2_shift,
    w_up,
    b_up,
    w_down,
    b_down,
):
    low = jnp.bfloat16
    slot_count, tok_dev, width = tokens_in.shape
    core, place = (lax.axis_index("core"), lax.axis_index("z"))
    depth = lax.axis_size("z")
    planes = lax.axis_size("y") * lax.axis_size("x")
    length = depth * tok_dev
    block = width // (2 * planes)
    part_rows = w_query.shape[0]
    half = width // 2
    ff_width = w_up.shape[1]
    ff_half = ff_width // 2
    ff_block = ff_width // (2 * planes)
    ff_rows = w_down.shape[0]

    def split_cols(value, size):
        lead = value.shape[:-1]
        view = value.reshape(lead + (-1, 2, size))
        even, odd = (view[..., 0, :], view[..., 1, :])
        mine = jnp.where(core == 0, even, odd)
        other = jnp.where(core == 0, odd, even)
        return (mine.reshape(lead + (-1,)), other.reshape(lead + (-1,)))

    def join_cols(mine, other, size):
        lead = mine.shape[:-1]
        view = lead + (-1, size)
        return in_order(core, mine.reshape(view), other.reshape(view), len(lead) + 1).reshape(
            lead + (-1,)
        )

    def to_image(local):
        mine, other = split_cols(local, block)
        images = in_order(core, mine, swap_core(other), 0)
        images = images.reshape(2 * slot_count, tok_dev, half)
        mine = trade_z(images).reshape(length, half)
        return join_cols(mine, swap_core(mine), block)

    def to_tokens(mine):
        images = trade_z(mine.reshape(depth, tok_dev, half))
        images = images.reshape(2, slot_count, tok_dev, half)
        other = swap_core(take(1 - core, images, 0))
        return join_cols(take(core, images, 0), other, block)

    vectors = (ln1_gain, ln1_shift, b_query, b_value, b_out, ln2_gain, ln2_shift, b_down)
    small = jnp.concatenate([vector.astype(low) for vector in vectors] + [b_up.astype(low)])
    small_rows = jnp.pad(small, (0, part_rows * 128 - small.shape[0])).reshape(part_rows, 128)

    project = gather_z(
        jnp.concatenate(
            [w_query.astype(low), w_key.astype(low), w_value.astype(low), small_rows], axis=1
        )
    )
    image_in = to_image(tokens_in)
    mine, other = split_cols(project[..., : 3 * width], block)
    small_part = project[..., 3 * width :]
    project_pair = in_order(
        core,
        jnp.concatenate([mine, small_part], axis=-1),
        swap_core(jnp.concatenate([other, small_part], axis=-1)),
        0,
    )
    project_all = gather_plane(project_pair.reshape(2 * depth * part_rows, 3 * half + 128))
    qkv_w = project_all[:, : 3 * half]
    small_all = project_all[:, 3 * half :].reshape(-1, part_rows * 128)[:, : small.shape[0]]
    small_all = small_all.astype(jnp.float32)
    count = len(vectors)
    wide = small_all[:, : count * part_rows].reshape(-1, count, part_rows)
    wide = wide.transpose(1, 0, 2).reshape(count, width)
    gain_one, shift_one, query_b, value_b, out_b, gain_two, shift_two, down_b = [
        wide[index] for index in range(count)
    ]
    query_b = split_cols(query_b, block)[0]
    value_b = split_cols(value_b, block)[0]
    up_b = split_cols(small_all[:, count * part_rows :].reshape(ff_width), ff_block)[0]

    out_mine = gather_plane(gather_z(w_out.astype(low)).reshape(depth * part_rows, width))
    out_other = swap_core(out_mine)

    up_part = gather_z(w_up.astype(low))
    mine, other = split_cols(up_part, ff_block)
    up_pair = in_order(core, mine, swap_core(other), 0)
    up_w = gather_plane(up_pair.reshape(2 * depth * part_rows, ff_half))
    down_w = gather_plane(gather_z(w_down.astype(low)).reshape(depth * ff_rows, width))

    live_slot = jnp.arange(slot_count) < group_count[0]
    live_low = live_slot.astype(low)[:, None, None]
    upstream_low = to_image(cotangent * live_low)

    owner, slot = (place // slot_count, place % slot_count)
    mask_mine = take(slot, key_mask, 0).astype(jnp.float32)[None, :]
    key_keep = jnp.where(core == owner, mask_mine, swap_core(mask_mine))[0]

    inputs = image_in.astype(jnp.float32)
    normal_one, inverse_one = norm_stats(inputs)
    normed_one = (normal_one * gain_one + shift_one).astype(low)
    qkv_b = jnp.concatenate([query_b, jnp.zeros_like(query_b), value_b])
    stacked = (product(normed_one, qkv_w) + qkv_b).astype(low).reshape(length, 3, half)
    mixed, log_total = attend_image((stacked, key_keep))
    mixed_other = swap_core(mixed)
    middle = inputs + (product(mixed, out_mine) + product(mixed_other, out_other)) + out_b
    normal_two, inverse_two = norm_stats(middle)
    normed_two = (normal_two * gain_two + shift_two).astype(low)
    hidden = product(normed_two, up_w) + up_b
    gate_sig = jax.nn.sigmoid(SLOPE * hidden)
    activated = (hidden * gate_sig).astype(low)
    grad_down = contract_rows(activated, upstream_low)
    grad_act = contract_cols(upstream_low, down_w)
    grad_hidden = (grad_act * (gate_sig + SLOPE * hidden * gate_sig * (1.0 - gate_sig))).astype(low)
    grad_two = contract_cols(grad_hidden, up_w)
    grad_normed_two = grad_two + swap_core(grad_two)
    grad_up = contract_rows(normed_two, grad_hidden)

    result = product(activated, down_w)
    mine, other = split_cols(result, block)
    result = split_cols(middle + down_b, block)[0] + (mine + swap_core(other))
    block_out = to_tokens(result.astype(low)) * live_low

    upstream = upstream_low.astype(jnp.float32)
    grad_mid, grad_gain_two, grad_shift_two = norm_back(
        grad_normed_two, normal_two, inverse_two, gain_two
    )
    grad_middle = upstream + grad_mid
    branch_low = grad_middle.astype(low)
    grad_mixed = contract_cols(branch_low, out_mine).astype(low)
    grad_out = contract_rows(mixed, branch_low)
    grad_stacked = attend_back((stacked, grad_mixed, log_total, key_keep))
    grad_qkv = grad_stacked.reshape(length, 3 * half)
    grad_project = contract_rows(normed_one, grad_qkv)

    grad_one = contract_cols(grad_qkv, qkv_w)
    scaled = grad_one * gain_one
    sums = jnp.concatenate(
        [
            jnp.sum(scaled, axis=1, keepdims=True),
            jnp.sum(scaled * normal_one, axis=1, keepdims=True),
        ],
        axis=1,
    )
    mine, other = split_cols(grad_one, block)
    got = swap_core(jnp.concatenate([other, jnp.pad(sums, ((0, 0), (0, 126)))], axis=1))
    grad_normed_one = mine + got[:, :half]
    means = (sums + got[:, half : half + 2]) / width
    normal_mine = split_cols(normal_one, block)[0]
    grad_first = inverse_one * (
        grad_normed_one * split_cols(gain_one, block)[0]
        - means[:, :1]
        - normal_mine * means[:, 1:]
    )
    input_grad = to_tokens((split_cols(grad_middle, block)[0] + grad_first).astype(low))

    grad_gain_one = jnp.sum(grad_normed_one * normal_mine, axis=0)
    grad_shift_one = jnp.sum(grad_normed_one, axis=0)
    bias_qkv = jnp.sum(grad_qkv.astype(jnp.float32), axis=0)
    small_grads = (
        grad_gain_one,
        grad_shift_one,
        bias_qkv[:half],
        bias_qkv[2 * half :],
        split_cols(jnp.sum(branch_low.astype(jnp.float32), axis=0), block)[0],
        split_cols(grad_gain_two, block)[0],
        split_cols(grad_shift_two, block)[0],
        split_cols(jnp.sum(upstream, axis=0), block)[0],
    )
    small_wide = jnp.stack(small_grads).reshape(count, planes * depth, part_rows)
    small_wide = small_wide.transpose(1, 0, 2).reshape(planes * depth, count * part_rows)
    grad_up_b = jnp.sum(grad_hidden.astype(jnp.float32), axis=0)
    small_wide = jnp.concatenate([small_wide, grad_up_b.reshape(planes * depth, -1)], axis=1)
    small_wide = jnp.pad(small_wide, ((0, 0), (0, part_rows * 128 - small.shape[0])))
    small_wide = jnp.broadcast_to(
        small_wide.reshape(planes, 1, depth * part_rows, 128),
        (planes, 2, depth * part_rows, 128),
    ).reshape(width, 128)

    down_rows = scatter_z(scatter_plane(grad_down).reshape(depth, ff_rows, width))

    def own_rows(total, cols, size):
        by_z = scatter_plane(total).reshape(2, depth, part_rows, cols).transpose(1, 0, 2, 3)
        pair = scatter_z(by_z)
        mine, other = (take(core, pair, 0), swap_core(take(1 - core, pair, 0)))
        return (mine, other)

    mine, other = own_rows(grad_up, ff_half, ff_block)
    up_rows = join_cols(mine, other, ff_block)
    out_rows = scatter_z(scatter_plane(grad_out).reshape(depth, part_rows, width))
    mine, other = own_rows(
        jnp.concatenate([grad_project, small_wide], axis=1), 3 * half + 128, block
    )
    project_rows = join_cols(mine[:, : 3 * half], other[:, : 3 * half], block)
    small_out = mine[:, 3 * half :].reshape(-1)[: small.shape[0]]
    pieces = [small_out[k * part_rows : (k + 1) * part_rows] for k in range(count)]
    return (
        block_out,
        input_grad,
        pieces[0],
        pieces[1],
        project_rows[:, :width],
        pieces[2],
        project_rows[:, width : 2 * width],
        project_rows[:, 2 * width :],
        pieces[3],
        out_rows,
        pieces[4],
        pieces[5],
        pieces[6],
        up_rows,
        small_out[count * part_rows :],
        down_rows,
        pieces[7],
    )


def solution(mesh):
    dp, seq = (mesh.shape["dp"], mesh.shape["seq"])
    function, axes, by_image, by_part = (per_device, mesh, "dp", ("dp", "seq"))
    by_token = "seq"
    if dp == 8 and seq == 4:
        function = own_image
        axes = jax.sharding.Mesh(mesh.devices.reshape(2, 2, 2, seq), ("y", "x", "core", "z"))
        by_image, by_token = (("y", "x", "core"), "z")
        by_part = ("y", "x", "core", "z")
    tokens, vector, matrix = (P(by_image, by_token, None), P(by_part), P(by_part, None))
    params = (
        (vector, vector, matrix, vector, matrix, matrix, vector, matrix)
        + (vector, vector, vector, matrix, vector, matrix, vector)
    )
    return jax.shard_map(
        function,
        mesh=axes,
        in_specs=(tokens, tokens, P(by_image), P(by_image, None)) + params,
        out_specs=(tokens, tokens) + params,
        check_vma=False,
    )
```

```python
import jax
import jax.numpy as jnp
from jax import lax
from jax.sharding import PartitionSpec as P

HD = 64


EPSILON = 1e-05
SLOPE = 1.702
MASKED = -1000000000.0


def norm_stats(values):
    center = values - jnp.mean(values, axis=-1, keepdims=True)
    inverse = lax.rsqrt(jnp.mean(center * center, axis=-1, keepdims=True) + EPSILON)
    return (center * inverse, inverse)


def norm_back(incoming, normal, inverse, gain):
    scaled = incoming * gain
    rows_grad = inverse * (
        scaled
        - jnp.mean(scaled, axis=-1, keepdims=True)
        - normal * jnp.mean(scaled * normal, axis=-1, keepdims=True)
    )
    return (rows_grad, jnp.sum(incoming * normal, axis=0), jnp.sum(incoming, axis=0))


def product(left, right):
    return jnp.dot(left, right, preferred_element_type=jnp.float32)


def contract_rows(left, right):
    return lax.dot_general(
        left, right, (((0,), (0,)), ((), ())), preferred_element_type=jnp.float32
    )


def contract_cols(left, right):
    return lax.dot_general(
        left, right, (((1,), (1,)), ((), ())), preferred_element_type=jnp.float32
    )


def split_heads(stacked):
    length = stacked.shape[0]
    heads_here = stacked.shape[2] // HD
    queries = stacked[:, 0].reshape(length, heads_here, HD)
    keys_all = stacked[:, 1].reshape(length, heads_here, HD)
    values_all = stacked[:, 2].reshape(length, heads_here, HD)
    return (queries, keys_all, values_all)


def masked_scores(queries, keys_all, key_keep):
    scores = jnp.einsum(
        "qhd,khd->hqk", queries, keys_all, preferred_element_type=jnp.float32
    ) * HD ** (-0.5)
    return jnp.where(key_keep[None, None, :] > 0, scores, MASKED)


def attend_image(paired):
    stacked, key_keep = paired
    queries, keys_all, values_all = split_heads(stacked)
    scores = masked_scores(queries, keys_all, key_keep)
    row_peak = jnp.max(scores, axis=-1, keepdims=True)
    weights_exp = jnp.exp(scores - row_peak)
    row_total = jnp.sum(weights_exp, axis=-1, keepdims=True)
    weights_soft = weights_exp / row_total
    mixed_out = jnp.einsum(
        "hqk,khd->qhd",
        weights_soft.astype(jnp.bfloat16),
        values_all,
        preferred_element_type=jnp.float32,
    )
    log_total = (row_peak + jnp.log(row_total))[..., 0]
    return (mixed_out.reshape(stacked.shape[0], stacked.shape[2]).astype(jnp.bfloat16), log_total)


def attend_back(packed):
    stacked, grad_mixed, log_total, key_keep = packed
    queries, keys_all, values_all = split_heads(stacked)
    scores = masked_scores(queries, keys_all, key_keep)
    weights_soft = jnp.exp(scores - log_total[..., None])
    grad_mix = grad_mixed.reshape(queries.shape)
    grad_values = jnp.einsum(
        "hqk,qhd->khd",
        weights_soft.astype(jnp.bfloat16),
        grad_mix,
        preferred_element_type=jnp.float32,
    )
    grad_weights = jnp.einsum(
        "qhd,khd->hqk", grad_mix, values_all, preferred_element_type=jnp.float32
    )
    row_inner = jnp.sum(grad_weights * weights_soft, axis=-1, keepdims=True)
    grad_scores = (weights_soft * (grad_weights - row_inner)).astype(jnp.bfloat16)
    grad_queries = jnp.einsum(
        "hqk,khd->qhd", grad_scores, keys_all, preferred_element_type=jnp.float32
    ) * HD ** (-0.5)
    grad_keys = jnp.einsum(
        "hqk,qhd->khd", grad_scores, queries, preferred_element_type=jnp.float32
    ) * HD ** (-0.5)
    length = stacked.shape[0]
    return jnp.stack(
        [
            grad_queries.reshape(length, -1),
            grad_keys.reshape(length, -1),
            grad_values.reshape(length, -1),
        ],
        axis=1,
    ).astype(jnp.bfloat16)


def per_device(
    tokens_in,
    cotangent,
    group_count,
    key_mask,
    ln1_gain,
    ln1_shift,
    w_query,
    b_query,
    w_key,
    w_value,
    b_value,
    w_out,
    b_out,
    ln2_gain,
    ln2_shift,
    w_up,
    b_up,
    w_down,
    b_down,
):
    slot_count, tok_dev, width = tokens_in.shape
    row_count = slot_count * tok_dev
    shared = (
        lax.all_gather(ln1_gain.astype(jnp.bfloat16), ("dp", "seq"), axis=0, tiled=True),
        lax.all_gather(ln1_shift.astype(jnp.bfloat16), ("dp", "seq"), axis=0, tiled=True),
        lax.all_gather(w_query.astype(jnp.bfloat16), ("dp", "seq"), axis=0, tiled=True),
        lax.all_gather(b_query.astype(jnp.bfloat16), ("dp", "seq"), axis=0, tiled=True),
        lax.all_gather(w_key.astype(jnp.bfloat16), ("dp", "seq"), axis=0, tiled=True),
        lax.all_gather(w_value.astype(jnp.bfloat16), ("dp", "seq"), axis=0, tiled=True),
        lax.all_gather(b_value.astype(jnp.bfloat16), ("dp", "seq"), axis=0, tiled=True),
        lax.all_gather(w_out.astype(jnp.bfloat16), ("dp", "seq"), axis=0, tiled=True),
        lax.all_gather(b_out.astype(jnp.bfloat16), ("dp", "seq"), axis=0, tiled=True),
        lax.all_gather(ln2_gain.astype(jnp.bfloat16), ("dp", "seq"), axis=0, tiled=True),
        lax.all_gather(ln2_shift.astype(jnp.bfloat16), ("dp", "seq"), axis=0, tiled=True),
        lax.all_gather(w_up.astype(jnp.bfloat16), ("dp", "seq"), axis=0, tiled=True),
        lax.all_gather(b_up.astype(jnp.bfloat16), ("dp", "seq"), axis=0, tiled=True),
        lax.all_gather(w_down.astype(jnp.bfloat16), ("dp", "seq"), axis=0, tiled=True),
        lax.all_gather(b_down.astype(jnp.bfloat16), ("dp", "seq"), axis=0, tiled=True),
    )
    (
        gain_one,
        shift_one,
        query_w,
        query_b,
        key_w,
        value_w,
        value_b,
        out_w,
        out_b,
        gain_two,
        shift_two,
        up_w,
        up_b,
        down_w,
        down_b,
    ) = shared
    live_slot = (jnp.arange(slot_count) < group_count[0]).astype(jnp.float32)[:, None, None]
    inputs = tokens_in.astype(jnp.float32).reshape(row_count, width)
    normal_one, inverse_one = norm_stats(inputs)
    normed_one = (normal_one * gain_one + shift_one).astype(jnp.bfloat16)
    queries = (product(normed_one, query_w) + query_b).astype(jnp.bfloat16)
    keys_all = product(normed_one, key_w).astype(jnp.bfloat16)
    values_all = (product(normed_one, value_w) + value_b).astype(jnp.bfloat16)
    stacked = jnp.stack([queries, keys_all, values_all], axis=1).reshape(
        slot_count, tok_dev, 3, width
    )
    by_heads = lax.all_to_all(stacked, "seq", split_axis=3, concat_axis=1, tiled=True)
    mixed_heads, log_total = lax.map(attend_image, (by_heads, key_mask))
    mixed_tok = lax.all_to_all(mixed_heads, "seq", split_axis=1, concat_axis=2, tiled=True).reshape(
        row_count, width
    )
    middle = inputs + product(mixed_tok, out_w) + out_b
    normal_two, inverse_two = norm_stats(middle)
    normed_two = (normal_two * gain_two + shift_two).astype(jnp.bfloat16)
    hidden = product(normed_two, up_w) + up_b
    gate_sig = jax.nn.sigmoid(SLOPE * hidden)
    activated = (hidden * gate_sig).astype(jnp.bfloat16)
    result = middle + product(activated, down_w) + down_b
    block_out = (result.reshape(slot_count, tok_dev, width) * live_slot).astype(jnp.bfloat16)
    upstream = (cotangent.astype(jnp.float32) * live_slot).reshape(row_count, width)
    upstream_low = upstream.astype(jnp.bfloat16)
    grad_down = contract_rows(activated, upstream_low)
    grad_down_b = jnp.sum(upstream, axis=0)
    grad_act = contract_cols(upstream_low, down_w)
    grad_hidden = (grad_act * (gate_sig + SLOPE * hidden * gate_sig * (1.0 - gate_sig))).astype(
        jnp.bfloat16
    )
    grad_up = contract_rows(normed_two, grad_hidden)
    grad_up_b = jnp.sum(grad_hidden.astype(jnp.float32), axis=0)
    grad_normed_two = contract_cols(grad_hidden, up_w)
    grad_mid, grad_gain_two, grad_shift_two = norm_back(
        grad_normed_two, normal_two, inverse_two, gain_two
    )
    grad_middle = upstream + grad_mid
    branch_low = grad_middle.astype(jnp.bfloat16)
    grad_out = contract_rows(mixed_tok, branch_low)
    grad_out_b = jnp.sum(branch_low.astype(jnp.float32), axis=0)
    grad_mixed = (
        contract_cols(branch_low, out_w).astype(jnp.bfloat16).reshape(slot_count, tok_dev, width)
    )
    grad_by_heads = lax.all_to_all(grad_mixed, "seq", split_axis=2, concat_axis=1, tiled=True)
    grad_stacked = lax.map(attend_back, (by_heads, grad_by_heads, log_total, key_mask))
    grad_tok = lax.all_to_all(grad_stacked, "seq", split_axis=1, concat_axis=3, tiled=True).reshape(
        row_count, 3, width
    )
    grad_q_rows = grad_tok[:, 0]
    grad_k_rows = grad_tok[:, 1]
    grad_v_rows = grad_tok[:, 2]
    grad_query = contract_rows(normed_one, grad_q_rows)
    grad_query_b = jnp.sum(grad_q_rows.astype(jnp.float32), axis=0)
    grad_key = contract_rows(normed_one, grad_k_rows)
    grad_value = contract_rows(normed_one, grad_v_rows)
    grad_value_b = jnp.sum(grad_v_rows.astype(jnp.float32), axis=0)
    grad_normed_one = (
        contract_cols(grad_q_rows, query_w)
        + contract_cols(grad_k_rows, key_w)
        + contract_cols(grad_v_rows, value_w)
    )
    grad_first, grad_gain_one, grad_shift_one = norm_back(
        grad_normed_one, normal_one, inverse_one, gain_one
    )
    input_grad = (grad_middle + grad_first).astype(jnp.bfloat16).reshape(slot_count, tok_dev, width)
    every_shard = (
        lax.psum_scatter(grad_gain_one, ("dp", "seq"), scatter_dimension=0, tiled=True),
        lax.psum_scatter(grad_shift_one, ("dp", "seq"), scatter_dimension=0, tiled=True),
        lax.psum_scatter(grad_query, ("dp", "seq"), scatter_dimension=0, tiled=True),
        lax.psum_scatter(grad_query_b, ("dp", "seq"), scatter_dimension=0, tiled=True),
        lax.psum_scatter(grad_key, ("dp", "seq"), scatter_dimension=0, tiled=True),
        lax.psum_scatter(grad_value, ("dp", "seq"), scatter_dimension=0, tiled=True),
        lax.psum_scatter(grad_value_b, ("dp", "seq"), scatter_dimension=0, tiled=True),
        lax.psum_scatter(grad_out, ("dp", "seq"), scatter_dimension=0, tiled=True),
        lax.psum_scatter(grad_out_b, ("dp", "seq"), scatter_dimension=0, tiled=True),
        lax.psum_scatter(grad_gain_two, ("dp", "seq"), scatter_dimension=0, tiled=True),
        lax.psum_scatter(grad_shift_two, ("dp", "seq"), scatter_dimension=0, tiled=True),
        lax.psum_scatter(grad_up, ("dp", "seq"), scatter_dimension=0, tiled=True),
        lax.psum_scatter(grad_up_b, ("dp", "seq"), scatter_dimension=0, tiled=True),
        lax.psum_scatter(grad_down, ("dp", "seq"), scatter_dimension=0, tiled=True),
        lax.psum_scatter(grad_down_b, ("dp", "seq"), scatter_dimension=0, tiled=True),
    )
    return (block_out, input_grad) + tuple(every_shard)


def swap_core(value):
    return lax.ppermute(value, "core", [(0, 1), (1, 0)])


def swap_x(value):
    return lax.ppermute(value, "x", [(0, 1), (1, 0)])


def swap_y(value):
    return lax.ppermute(value, "y", [(0, 1), (1, 0)])


def trade_z(value):
    return lax.all_to_all(value, "z", split_axis=0, concat_axis=0, tiled=True)


def in_order(index, mine, other, axis):
    return jnp.where(
        index == 0, jnp.stack([mine, other], axis=axis), jnp.stack([other, mine], axis=axis)
    )


def side_by_side(index, mine, other):
    return jnp.where(
        index == 0,
        jnp.concatenate([mine, other], axis=-1),
        jnp.concatenate([other, mine], axis=-1),
    )


def half_cols(index, value):
    middle = value.shape[-1] // 2
    return jnp.where(index == 0, value[..., :middle], value[..., middle:])


def take(index, value):
    return lax.dynamic_index_in_dim(value, index, 0, keepdims=False)


def after(value, *earlier):
    return lax.optimization_barrier((value,) + earlier)[0]


def parity_cols(value, size):
    count = value.shape[-1] // size
    parts = [value[..., k * size : (k + 1) * size] for k in range(count)]
    return parts[0::2] + parts[1::2]


def natural_cols(even, odd, size):
    parts = []
    for k in range(even.shape[-1] // size):
        parts += [even[..., k * size : (k + 1) * size], odd[..., k * size : (k + 1) * size]]
    return jnp.concatenate(parts, axis=-1)


def gather_z(shard):
    copies = lax.axis_size("z")
    return trade_z(jnp.broadcast_to(shard[None], (copies,) + shard.shape))


def gather_plane(rows):
    here_x, here_y = (lax.axis_index("x"), lax.axis_index("y"))
    half = rows.shape[0] // 2
    first, second = (rows[:half], rows[half:])
    first_x = swap_x(first)
    second_y = swap_y(second)
    first_pair = in_order(here_x, first, first_x, 0)
    second_pair = in_order(here_y, second, second_y, 0)
    first_y = swap_y(first_pair)
    second_x = swap_x(second_pair)
    first_all = in_order(here_y, first_pair, first_y, 0)
    second_all = in_order(here_x, second_pair, second_x, 1)
    return jnp.stack([first_all, second_all], axis=2).reshape(4 * rows.shape[0], rows.shape[1])


def scatter_plane(left, right):
    low = jnp.bfloat16
    here_x, here_y = (lax.axis_index("x"), lax.axis_index("y"))
    rows = left.shape[1] // 4
    cols = right.shape[1] // 2
    first, second = (right[:, :cols], right[:, cols:])

    def along_x(index):
        return jnp.concatenate(
            [half_cols(index, left[:, : 2 * rows]), half_cols(index, left[:, 2 * rows :])], axis=1
        )

    first_got = swap_y(contract_rows(half_cols(1 - here_y, left), first).astype(low))
    second_got = swap_x(contract_rows(along_x(1 - here_x), second).astype(low))
    first_sum = contract_rows(half_cols(here_y, left), first) + first_got
    second_sum = contract_rows(along_x(here_x), second) + second_got
    first_sum = first_sum.reshape(2, rows, cols)
    second_sum = second_sum.reshape(2, rows, cols)
    first_last = swap_x(take(1 - here_x, first_sum).astype(low))
    second_last = swap_y(take(1 - here_y, second_sum).astype(low))
    return (take(here_x, first_sum) + first_last, take(here_y, second_sum) + second_last)


def scatter_z(parts):
    return jnp.sum(trade_z(parts.astype(jnp.bfloat16)).astype(jnp.float32), axis=0)


def own_image(
    tokens_in,
    cotangent,
    group_count,
    key_mask,
    ln1_gain,
    ln1_shift,
    w_query,
    b_query,
    w_key,
    w_value,
    b_value,
    w_out,
    b_out,
    ln2_gain,
    ln2_shift,
    w_up,
    b_up,
    w_down,
    b_down,
):
    low = jnp.bfloat16
    slot_count, tok_dev, width = tokens_in.shape
    core, place = (lax.axis_index("core"), lax.axis_index("z"))
    here_x, here_y = (lax.axis_index("x"), lax.axis_index("y"))
    depth = lax.axis_size("z")
    planes = 4
    length = depth * tok_dev
    block = width // (2 * planes)
    part_rows = w_query.shape[0]
    half = width // 2
    ff_half = w_up.shape[1] // 2
    ff_block = ff_half // planes
    ff_rows = w_down.shape[0]
    count = 8
    small_size = count * part_rows + b_up.shape[0]

    def to_image(local, *earlier):
        images = in_order(
            core, half_cols(core, local), swap_core(half_cols(1 - core, local)), 0
        ).reshape(2 * slot_count, tok_dev, half)
        mine = trade_z(after(images, *earlier)).reshape(length, half)
        return (side_by_side(core, mine, swap_core(mine)), mine)

    def to_tokens(mine):
        images = trade_z(mine.reshape(depth, tok_dev, half))
        images = images.reshape(2, slot_count, tok_dev, half)
        return side_by_side(core, take(core, images), swap_core(take(1 - core, images)))

    vectors = (ln1_gain, ln1_shift, b_query, b_value, b_out, ln2_gain, ln2_shift, b_down, b_up)
    small = jnp.concatenate([vector.astype(low) for vector in vectors])
    small_rows = jnp.pad(small, (0, part_rows * 128 - small_size)).reshape(part_rows, 128)
    columns = [parity_cols(w, block) for w in (w_query, w_key, w_value)]
    evens = [part for parts in columns for part in parts[:planes]]
    odds = [part for parts in columns for part in parts[planes:]]
    project = gather_z(
        jnp.concatenate([part.astype(low) for part in evens + odds] + [small_rows], axis=1)
    )

    up_local = jnp.concatenate([part.astype(low) for part in parity_cols(w_up, ff_block)], axis=1)
    up_pair = in_order(core, half_cols(core, up_local), swap_core(half_cols(1 - core, up_local)), 0)
    up_pair = up_pair.reshape(2 * part_rows, ff_half)
    shard = jnp.concatenate(
        [w_down.astype(low), up_pair[:, :width], up_pair[:, width:], w_out.astype(low)], axis=0
    )
    gathered = lax.all_gather(shard, ("y", "x", "z"), axis=0, tiled=False)

    image_in, token_half = to_image(tokens_in, project)
    small_part = project[..., 6 * half :]
    project_pair = in_order(
        core,
        jnp.concatenate([half_cols(core, project[..., : 6 * half]), small_part], axis=-1),
        swap_core(
            jnp.concatenate([half_cols(1 - core, project[..., : 6 * half]), small_part], axis=-1)
        ),
        0,
    )
    project_all = gather_plane(project_pair.reshape(2 * depth * part_rows, 3 * half + 128))
    qkv_w = project_all[:, : 3 * half]
    small_all = project_all[:, 3 * half :].reshape(-1, part_rows * 128)[:, :small_size]
    small_all = small_all.astype(jnp.float32)
    wide = small_all[:, : count * part_rows].reshape(-1, count, part_rows)
    wide = wide.transpose(1, 0, 2).reshape(count, width)
    gain_one, shift_one, query_b, value_b, out_b, gain_two, shift_two, down_b = [
        wide[index] for index in range(count)
    ]

    def own_cols(vector, size):
        return jnp.where(
            core == 0,
            jnp.concatenate(parity_cols(vector, size)[:planes]),
            jnp.concatenate(parity_cols(vector, size)[planes:]),
        )

    query_b = own_cols(query_b, block)
    value_b = own_cols(value_b, block)
    up_b = own_cols(small_all[:, count * part_rows :].reshape(2 * ff_half), ff_block)

    down_w = gathered[:, :ff_rows].reshape(ff_half, width)

    def by_feature(rows):
        return (
            rows.reshape(planes, depth, 2, part_rows, width)
            .transpose(0, 2, 1, 3, 4)
            .reshape(width, width)
        )

    up_w = jnp.concatenate(
        [
            by_feature(gathered[:, ff_rows : ff_rows + 2 * part_rows]),
            by_feature(gathered[:, ff_rows + 2 * part_rows : ff_rows + 4 * part_rows]),
        ],
        axis=1,
    )
    out_mine = gathered[:, ff_rows + 4 * part_rows :].reshape(half, width)
    out_other = swap_core(out_mine)

    live_slot = jnp.arange(slot_count) < group_count[0]
    live_low = live_slot.astype(low)[:, None, None]
    upstream_low, upstream_half = to_image(cotangent * live_low, image_in)

    owner, slot = (place // slot_count, place % slot_count)
    mask_mine = take(slot, key_mask).astype(jnp.float32)[None, :]
    key_keep = jnp.where(core == owner, mask_mine, swap_core(mask_mine))[0]

    inputs = image_in.astype(jnp.float32)
    normal_one, inverse_one = norm_stats(inputs)
    normed_one = (normal_one * gain_one + shift_one).astype(low)
    qkv_b = jnp.concatenate([query_b, jnp.zeros_like(query_b), value_b])
    stacked = (product(normed_one, qkv_w) + qkv_b).astype(low).reshape(length, 3, half)
    mixed, log_total = attend_image((stacked, key_keep))
    mixed_other = swap_core(mixed)
    middle = inputs + (product(mixed, out_mine) + product(mixed_other, out_other)) + out_b
    normal_two, inverse_two = norm_stats(middle)
    normed_two = (normal_two * gain_two + shift_two).astype(low)
    hidden = product(normed_two, up_w) + up_b
    gate_sig = jax.nn.sigmoid(SLOPE * hidden)
    activated = (hidden * gate_sig).astype(low)
    down_first, down_second = scatter_plane(activated, upstream_low)
    grad_act = contract_cols(upstream_low, down_w)
    grad_hidden = (grad_act * (gate_sig + SLOPE * hidden * gate_sig * (1.0 - gate_sig))).astype(low)
    grad_two = contract_cols(grad_hidden, up_w)
    grad_normed_two = grad_two + swap_core(grad_two)
    up_first, up_second = scatter_plane(normed_two, grad_hidden)

    result = product(activated, down_w)
    result = half_cols(core, middle + down_b) + (
        half_cols(core, result) + swap_core(half_cols(1 - core, result))
    )
    block_out = to_tokens(result.astype(low)) * live_low

    upstream = upstream_low.astype(jnp.float32)
    grad_mid, grad_gain_two, grad_shift_two = norm_back(
        grad_normed_two, normal_two, inverse_two, gain_two
    )
    grad_middle = upstream + grad_mid
    branch_low = grad_middle.astype(low)
    grad_mixed = contract_cols(branch_low, out_mine).astype(low)
    out_first, out_second = scatter_plane(mixed, branch_low)
    grad_stacked = attend_back((stacked, grad_mixed, log_total, key_keep))
    grad_qkv = grad_stacked.reshape(length, 3 * half)
    project_first, project_second = scatter_plane(normed_one, grad_qkv)

    grad_one = contract_cols(grad_qkv, qkv_w)
    scaled = grad_one * gain_one
    sums = jnp.concatenate(
        [
            jnp.sum(scaled, axis=1, keepdims=True),
            jnp.sum(scaled * normal_one, axis=1, keepdims=True),
        ],
        axis=1,
    )
    got = swap_core(
        jnp.concatenate(
            [half_cols(1 - core, grad_one), jnp.pad(sums, ((0, 0), (0, 126)))], axis=1
        )
    )
    grad_normed_one = half_cols(core, grad_one) + got[:, :half]
    means = (sums + got[:, half : half + 2]) / width
    normal_mine = half_cols(core, normal_one)
    grad_first = inverse_one * (
        grad_normed_one * half_cols(core, gain_one) - means[:, :1] - normal_mine * means[:, 1:]
    )
    input_grad = to_tokens((half_cols(core, grad_middle) + grad_first).astype(low))

    bias_qkv = jnp.sum(grad_qkv.astype(jnp.float32), axis=0)

    def placed(mine):
        none = jnp.zeros_like(mine)
        return side_by_side(core, mine, none)

    def spread(mine):
        none = jnp.zeros_like(mine)
        return jnp.where(
            core == 0, natural_cols(mine, none, block), natural_cols(none, mine, block)
        )

    first_core = (core == 0).astype(jnp.float32)
    small_grads = jnp.stack(
        [
            placed(jnp.sum(grad_normed_one * normal_mine, axis=0)),
            placed(jnp.sum(grad_normed_one, axis=0)),
            spread(bias_qkv[:half]),
            spread(bias_qkv[2 * half :]),
            first_core * jnp.sum(branch_low.astype(jnp.float32), axis=0),
            first_core * grad_gain_two,
            first_core * grad_shift_two,
            placed(jnp.sum(upstream_half.astype(jnp.float32), axis=0)),
        ]
    )
    small_wide = small_grads.reshape(count, 2 * planes * depth, part_rows)
    small_wide = small_wide.transpose(1, 0, 2).reshape(planes, 2, depth, count * part_rows)
    grad_up_b = jnp.sum(grad_hidden.astype(jnp.float32), axis=0).reshape(planes, depth, -1)
    grad_up_b = in_order(core, grad_up_b, jnp.zeros_like(grad_up_b), 1)
    small_wide = jnp.concatenate([small_wide, grad_up_b], axis=-1).reshape(2, 2, -1)
    small_sum = take(here_y, small_wide) + swap_y(take(1 - here_y, small_wide))
    small_sum = take(here_x, small_sum) + swap_x(take(1 - here_x, small_sum))
    small_sum = small_sum.reshape(2, depth, small_size).transpose(1, 0, 2)
    small_sum = jnp.pad(small_sum, ((0, 0), (0, 0), (0, part_rows * 128 - small_size)))
    small_sum = small_sum.reshape(depth, 2, part_rows, 128)

    down_rows = scatter_z(
        jnp.concatenate([down_first, down_second], axis=1).reshape(depth, ff_rows, width)
    )

    def by_place(rows):
        return rows.reshape(2, depth, part_rows, -1).transpose(1, 0, 2, 3)

    wide_parts = scatter_z(
        jnp.concatenate(
            [
                by_place(up_first).reshape(depth, 2 * part_rows, width),
                by_place(up_second).reshape(depth, 2 * part_rows, width),
                jnp.concatenate([out_first, out_second], axis=1).reshape(depth, part_rows, width),
            ],
            axis=1,
        )
    )
    out_rows = wide_parts[4 * part_rows :]
    up_pair = jnp.concatenate(
        [wide_parts[: 2 * part_rows], wide_parts[2 * part_rows : 4 * part_rows]], axis=1
    ).reshape(2, part_rows, ff_half)
    mine, other = (take(core, up_pair), swap_core(take(1 - core, up_pair)))
    up_rows = natural_cols(
        jnp.where(core == 0, mine, other), jnp.where(core == 0, other, mine), ff_block
    )

    project_pair = scatter_z(
        jnp.concatenate([by_place(project_first), by_place(project_second), small_sum], axis=-1)
    )
    mine, other = (take(core, project_pair), swap_core(take(1 - core, project_pair)))
    even = jnp.where(core == 0, mine, other)
    odd = jnp.where(core == 0, other, mine)
    query_rows, key_rows, value_rows = [
        natural_cols(even[:, k * half : (k + 1) * half], odd[:, k * half : (k + 1) * half], block)
        for k in range(3)
    ]
    small_out = (mine[:, 3 * half :] + other[:, 3 * half :]).reshape(-1)
    pieces = [small_out[k * part_rows : (k + 1) * part_rows] for k in range(count)]
    return (
        block_out,
        input_grad,
        pieces[0],
        pieces[1],
        query_rows,
        pieces[2],
        key_rows,
        value_rows,
        pieces[3],
        out_rows,
        pieces[4],
        pieces[5],
        pieces[6],
        up_rows,
        small_out[count * part_rows : small_size],
        down_rows,
        pieces[7],
    )


def solution(mesh):
    dp, seq = (mesh.shape["dp"], mesh.shape["seq"])
    function, axes, by_image, by_part = (per_device, mesh, "dp", ("dp", "seq"))
    by_token = "seq"
    if dp == 8 and seq == 4:
        function = own_image
        axes = jax.sharding.Mesh(mesh.devices.reshape(2, 2, 2, seq), ("y", "x", "core", "z"))
        by_image, by_token = (("y", "x", "core"), "z")
        by_part = ("y", "x", "core", "z")
    tokens, vector, matrix = (P(by_image, by_token, None), P(by_part), P(by_part, None))
    params = (
        (vector, vector, matrix, vector, matrix, matrix, vector, matrix)
        + (vector, vector, vector, matrix, vector, matrix, vector)
    )
    return jax.shard_map(
        function,
        mesh=axes,
        in_specs=(tokens, tokens, P(by_image), P(by_image, None)) + params,
        out_specs=(tokens, tokens) + params,
        check_vma=False,
    )
```

```python
import jax
import jax.numpy as jnp
from jax import lax
from jax.experimental import pallas as pl
from jax.sharding import PartitionSpec as P


HD = 64


EPSILON = 1e-05
SLOPE = 1.702
MASKED = -1000000000.0


def norm_stats(values):
    center = values - jnp.mean(values, axis=-1, keepdims=True)
    inverse = lax.rsqrt(jnp.mean(center * center, axis=-1, keepdims=True) + EPSILON)
    return (center * inverse, inverse)


def norm_back(incoming, normal, inverse, gain):
    scaled = incoming * gain
    rows_grad = inverse * (
        scaled
        - jnp.mean(scaled, axis=-1, keepdims=True)
        - normal * jnp.mean(scaled * normal, axis=-1, keepdims=True)
    )
    return (rows_grad, jnp.sum(incoming * normal, axis=0), jnp.sum(incoming, axis=0))


def product(left, right):
    return jnp.dot(left, right, preferred_element_type=jnp.float32)


def contract_rows(left, right):
    return lax.dot_general(
        left, right, (((0,), (0,)), ((), ())), preferred_element_type=jnp.float32
    )


def contract_cols(left, right):
    return lax.dot_general(
        left, right, (((1,), (1,)), ((), ())), preferred_element_type=jnp.float32
    )


def split_heads(stacked):
    length = stacked.shape[0]
    heads_here = stacked.shape[2] // HD
    queries = stacked[:, 0].reshape(length, heads_here, HD)
    keys_all = stacked[:, 1].reshape(length, heads_here, HD)
    values_all = stacked[:, 2].reshape(length, heads_here, HD)
    return (queries, keys_all, values_all)


def masked_scores(queries, keys_all, key_keep):
    scores = jnp.einsum(
        "qhd,khd->hqk", queries, keys_all, preferred_element_type=jnp.float32
    ) * HD ** (-0.5)
    return jnp.where(key_keep[None, None, :] > 0, scores, MASKED)


def attend_image(paired):
    stacked, key_keep = paired
    queries, keys_all, values_all = split_heads(stacked)
    scores = masked_scores(queries, keys_all, key_keep)
    row_peak = jnp.max(scores, axis=-1, keepdims=True)
    weights_exp = jnp.exp(scores - row_peak)
    row_total = jnp.sum(weights_exp, axis=-1, keepdims=True)
    weights_soft = weights_exp / row_total
    mixed_out = jnp.einsum(
        "hqk,khd->qhd",
        weights_soft.astype(jnp.bfloat16),
        values_all,
        preferred_element_type=jnp.float32,
    )
    log_total = (row_peak + jnp.log(row_total))[..., 0]
    return (mixed_out.reshape(stacked.shape[0], stacked.shape[2]).astype(jnp.bfloat16), log_total)


def attend_back(packed):
    stacked, grad_mixed, log_total, key_keep = packed
    queries, keys_all, values_all = split_heads(stacked)
    scores = masked_scores(queries, keys_all, key_keep)
    weights_soft = jnp.exp(scores - log_total[..., None])
    grad_mix = grad_mixed.reshape(queries.shape)
    grad_values = jnp.einsum(
        "hqk,qhd->khd",
        weights_soft.astype(jnp.bfloat16),
        grad_mix,
        preferred_element_type=jnp.float32,
    )
    grad_weights = jnp.einsum(
        "qhd,khd->hqk", grad_mix, values_all, preferred_element_type=jnp.float32
    )
    row_inner = jnp.sum(grad_weights * weights_soft, axis=-1, keepdims=True)
    grad_scores = (weights_soft * (grad_weights - row_inner)).astype(jnp.bfloat16)
    grad_queries = jnp.einsum(
        "hqk,khd->qhd", grad_scores, keys_all, preferred_element_type=jnp.float32
    ) * HD ** (-0.5)
    grad_keys = jnp.einsum(
        "hqk,qhd->khd", grad_scores, queries, preferred_element_type=jnp.float32
    ) * HD ** (-0.5)
    length = stacked.shape[0]
    return jnp.stack(
        [
            grad_queries.reshape(length, -1),
            grad_keys.reshape(length, -1),
            grad_values.reshape(length, -1),
        ],
        axis=1,
    ).astype(jnp.bfloat16)


def per_device(
    tokens_in,
    cotangent,
    group_count,
    key_mask,
    ln1_gain,
    ln1_shift,
    w_query,
    b_query,
    w_key,
    w_value,
    b_value,
    w_out,
    b_out,
    ln2_gain,
    ln2_shift,
    w_up,
    b_up,
    w_down,
    b_down,
):
    slot_count, tok_dev, width = tokens_in.shape
    row_count = slot_count * tok_dev
    shared = (
        lax.all_gather(ln1_gain.astype(jnp.bfloat16), ("dp", "seq"), axis=0, tiled=True),
        lax.all_gather(ln1_shift.astype(jnp.bfloat16), ("dp", "seq"), axis=0, tiled=True),
        lax.all_gather(w_query.astype(jnp.bfloat16), ("dp", "seq"), axis=0, tiled=True),
        lax.all_gather(b_query.astype(jnp.bfloat16), ("dp", "seq"), axis=0, tiled=True),
        lax.all_gather(w_key.astype(jnp.bfloat16), ("dp", "seq"), axis=0, tiled=True),
        lax.all_gather(w_value.astype(jnp.bfloat16), ("dp", "seq"), axis=0, tiled=True),
        lax.all_gather(b_value.astype(jnp.bfloat16), ("dp", "seq"), axis=0, tiled=True),
        lax.all_gather(w_out.astype(jnp.bfloat16), ("dp", "seq"), axis=0, tiled=True),
        lax.all_gather(b_out.astype(jnp.bfloat16), ("dp", "seq"), axis=0, tiled=True),
        lax.all_gather(ln2_gain.astype(jnp.bfloat16), ("dp", "seq"), axis=0, tiled=True),
        lax.all_gather(ln2_shift.astype(jnp.bfloat16), ("dp", "seq"), axis=0, tiled=True),
        lax.all_gather(w_up.astype(jnp.bfloat16), ("dp", "seq"), axis=0, tiled=True),
        lax.all_gather(b_up.astype(jnp.bfloat16), ("dp", "seq"), axis=0, tiled=True),
        lax.all_gather(w_down.astype(jnp.bfloat16), ("dp", "seq"), axis=0, tiled=True),
        lax.all_gather(b_down.astype(jnp.bfloat16), ("dp", "seq"), axis=0, tiled=True),
    )
    (
        gain_one,
        shift_one,
        query_w,
        query_b,
        key_w,
        value_w,
        value_b,
        out_w,
        out_b,
        gain_two,
        shift_two,
        up_w,
        up_b,
        down_w,
        down_b,
    ) = shared
    live_slot = (jnp.arange(slot_count) < group_count[0]).astype(jnp.float32)[:, None, None]
    inputs = tokens_in.astype(jnp.float32).reshape(row_count, width)
    normal_one, inverse_one = norm_stats(inputs)
    normed_one = (normal_one * gain_one + shift_one).astype(jnp.bfloat16)
    queries = (product(normed_one, query_w) + query_b).astype(jnp.bfloat16)
    keys_all = product(normed_one, key_w).astype(jnp.bfloat16)
    values_all = (product(normed_one, value_w) + value_b).astype(jnp.bfloat16)
    stacked = jnp.stack([queries, keys_all, values_all], axis=1).reshape(
        slot_count, tok_dev, 3, width
    )
    by_heads = lax.all_to_all(stacked, "seq", split_axis=3, concat_axis=1, tiled=True)
    mixed_heads, log_total = lax.map(attend_image, (by_heads, key_mask))
    mixed_tok = lax.all_to_all(mixed_heads, "seq", split_axis=1, concat_axis=2, tiled=True).reshape(
        row_count, width
    )
    middle = inputs + product(mixed_tok, out_w) + out_b
    normal_two, inverse_two = norm_stats(middle)
    normed_two = (normal_two * gain_two + shift_two).astype(jnp.bfloat16)
    hidden = product(normed_two, up_w) + up_b
    gate_sig = jax.nn.sigmoid(SLOPE * hidden)
    activated = (hidden * gate_sig).astype(jnp.bfloat16)
    result = middle + product(activated, down_w) + down_b
    block_out = (result.reshape(slot_count, tok_dev, width) * live_slot).astype(jnp.bfloat16)
    upstream = (cotangent.astype(jnp.float32) * live_slot).reshape(row_count, width)
    upstream_low = upstream.astype(jnp.bfloat16)
    grad_down = contract_rows(activated, upstream_low)
    grad_down_b = jnp.sum(upstream, axis=0)
    grad_act = contract_cols(upstream_low, down_w)
    grad_hidden = (grad_act * (gate_sig + SLOPE * hidden * gate_sig * (1.0 - gate_sig))).astype(
        jnp.bfloat16
    )
    grad_up = contract_rows(normed_two, grad_hidden)
    grad_up_b = jnp.sum(grad_hidden.astype(jnp.float32), axis=0)
    grad_normed_two = contract_cols(grad_hidden, up_w)
    grad_mid, grad_gain_two, grad_shift_two = norm_back(
        grad_normed_two, normal_two, inverse_two, gain_two
    )
    grad_middle = upstream + grad_mid
    branch_low = grad_middle.astype(jnp.bfloat16)
    grad_out = contract_rows(mixed_tok, branch_low)
    grad_out_b = jnp.sum(branch_low.astype(jnp.float32), axis=0)
    grad_mixed = (
        contract_cols(branch_low, out_w).astype(jnp.bfloat16).reshape(slot_count, tok_dev, width)
    )
    grad_by_heads = lax.all_to_all(grad_mixed, "seq", split_axis=2, concat_axis=1, tiled=True)
    grad_stacked = lax.map(attend_back, (by_heads, grad_by_heads, log_total, key_mask))
    grad_tok = lax.all_to_all(grad_stacked, "seq", split_axis=1, concat_axis=3, tiled=True).reshape(
        row_count, 3, width
    )
    grad_q_rows = grad_tok[:, 0]
    grad_k_rows = grad_tok[:, 1]
    grad_v_rows = grad_tok[:, 2]
    grad_query = contract_rows(normed_one, grad_q_rows)
    grad_query_b = jnp.sum(grad_q_rows.astype(jnp.float32), axis=0)
    grad_key = contract_rows(normed_one, grad_k_rows)
    grad_value = contract_rows(normed_one, grad_v_rows)
    grad_value_b = jnp.sum(grad_v_rows.astype(jnp.float32), axis=0)
    grad_normed_one = (
        contract_cols(grad_q_rows, query_w)
        + contract_cols(grad_k_rows, key_w)
        + contract_cols(grad_v_rows, value_w)
    )
    grad_first, grad_gain_one, grad_shift_one = norm_back(
        grad_normed_one, normal_one, inverse_one, gain_one
    )
    input_grad = (grad_middle + grad_first).astype(jnp.bfloat16).reshape(slot_count, tok_dev, width)
    every_shard = (
        lax.psum_scatter(grad_gain_one, ("dp", "seq"), scatter_dimension=0, tiled=True),
        lax.psum_scatter(grad_shift_one, ("dp", "seq"), scatter_dimension=0, tiled=True),
        lax.psum_scatter(grad_query, ("dp", "seq"), scatter_dimension=0, tiled=True),
        lax.psum_scatter(grad_query_b, ("dp", "seq"), scatter_dimension=0, tiled=True),
        lax.psum_scatter(grad_key, ("dp", "seq"), scatter_dimension=0, tiled=True),
        lax.psum_scatter(grad_value, ("dp", "seq"), scatter_dimension=0, tiled=True),
        lax.psum_scatter(grad_value_b, ("dp", "seq"), scatter_dimension=0, tiled=True),
        lax.psum_scatter(grad_out, ("dp", "seq"), scatter_dimension=0, tiled=True),
        lax.psum_scatter(grad_out_b, ("dp", "seq"), scatter_dimension=0, tiled=True),
        lax.psum_scatter(grad_gain_two, ("dp", "seq"), scatter_dimension=0, tiled=True),
        lax.psum_scatter(grad_shift_two, ("dp", "seq"), scatter_dimension=0, tiled=True),
        lax.psum_scatter(grad_up, ("dp", "seq"), scatter_dimension=0, tiled=True),
        lax.psum_scatter(grad_up_b, ("dp", "seq"), scatter_dimension=0, tiled=True),
        lax.psum_scatter(grad_down, ("dp", "seq"), scatter_dimension=0, tiled=True),
        lax.psum_scatter(grad_down_b, ("dp", "seq"), scatter_dimension=0, tiled=True),
    )
    return (block_out, input_grad) + tuple(every_shard)


def swap_core(value):
    return lax.ppermute(value, "core", [(0, 1), (1, 0)])


def swap_x(value):
    return lax.ppermute(value, "x", [(0, 1), (1, 0)])


def swap_y(value):
    return lax.ppermute(value, "y", [(0, 1), (1, 0)])


def trade_z(value):
    return lax.all_to_all(value, "z", split_axis=0, concat_axis=0, tiled=True)


def in_order(index, mine, other, axis):
    return jnp.where(
        index == 0, jnp.stack([mine, other], axis=axis), jnp.stack([other, mine], axis=axis)
    )


def side_by_side(index, mine, other):
    return jnp.where(
        index == 0,
        jnp.concatenate([mine, other], axis=-1),
        jnp.concatenate([other, mine], axis=-1),
    )


def half_cols(index, value):
    middle = value.shape[-1] // 2
    return jnp.where(index == 0, value[..., :middle], value[..., middle:])


def take(index, value):
    return lax.dynamic_index_in_dim(value, index, 0, keepdims=False)


def after(value, *earlier):
    return lax.optimization_barrier((value,) + earlier)[0]


def parity_cols(value, size):
    count = value.shape[-1] // size
    parts = [value[..., k * size : (k + 1) * size] for k in range(count)]
    return parts[0::2] + parts[1::2]


def natural_cols(even, odd, size):
    parts = []
    for k in range(even.shape[-1] // size):
        parts += [even[..., k * size : (k + 1) * size], odd[..., k * size : (k + 1) * size]]
    return jnp.concatenate(parts, axis=-1)


def gather_z(shard):
    copies = lax.axis_size("z")
    return trade_z(jnp.broadcast_to(shard[None], (copies,) + shard.shape))


def gather_plane(rows):
    here_x, here_y = (lax.axis_index("x"), lax.axis_index("y"))
    half = rows.shape[0] // 2
    first, second = (rows[:half], rows[half:])
    first_x = swap_x(first)
    second_y = swap_y(second)
    first_pair = in_order(here_x, first, first_x, 0)
    second_pair = in_order(here_y, second, second_y, 0)
    first_y = swap_y(first_pair)
    second_x = swap_x(second_pair)
    first_all = in_order(here_y, first_pair, first_y, 0)
    second_all = in_order(here_x, second_pair, second_x, 1)
    return jnp.stack([first_all, second_all], axis=2).reshape(4 * rows.shape[0], rows.shape[1])


def along_y(index, value):
    return half_cols(index, value)


def along_x(index, value):
    middle = value.shape[1] // 2
    return jnp.concatenate(
        [half_cols(index, value[:, :middle]), half_cols(index, value[:, middle:])], axis=1
    )


def scatter_start(pick, index, swap, left, right):
    sent = contract_rows(pick(1 - index, left), right).astype(jnp.bfloat16)
    return (swap(sent), sent)


def scatter_next(pick, index, next_index, swap, left, right, got):
    total = contract_rows(pick(index, left), right) + got
    total = total.reshape(2, total.shape[0] // 2, total.shape[1])
    sent = take(1 - next_index, total).astype(jnp.bfloat16)
    return (take(next_index, total), swap(sent), sent)


def lane_parts(value):
    lane = lax.broadcasted_iota(jnp.int32, value.shape, 1)
    none = jnp.zeros_like(value)
    return (jnp.where(lane < HD, value, none), jnp.where(lane < HD, none, value))


def attend_kernel(q_ref, k_ref, v_ref, keep_ref, out_ref):
    keys_all = k_ref[...]
    keep = keep_ref[...] > 0
    total = None
    for queries, values in zip(lane_parts(q_ref[...] * HD ** (-0.5)), lane_parts(v_ref[...])):
        scores = contract_cols(queries, keys_all)
        scores = jnp.where(keep, scores, MASKED)
        weights = jnp.exp(scores - jnp.max(scores, axis=1, keepdims=True))
        weights = weights * (1.0 / jnp.sum(weights, axis=1, keepdims=True))
        part = product(weights.astype(jnp.bfloat16), values)
        total = part if total is None else total + part
    out_ref[...] = total.astype(jnp.bfloat16)


def group_block(first, part):
    return lambda j: (0, (first + j) // 2 * 6 + 2 * part + (first + j) % 2)


def attend(stacked, key_keep):
    length, pairs = (stacked.shape[0], stacked.shape[1] // 384)
    columns = [pl.BlockSpec((length, 128), group_block(0, part)) for part in range(3)]
    return pl.pallas_call(
        attend_kernel,
        grid=(pairs,),
        in_specs=columns + [pl.BlockSpec((1, length), lambda j: (0, 0))],
        out_specs=pl.BlockSpec((length, 128), lambda j: (0, j)),
        out_shape=jax.ShapeDtypeStruct((length, pairs * 128), jnp.bfloat16),
        name="attend",
    )(stacked, stacked, stacked, key_keep)


def attend_back_kernel(q_ref, k_ref, v_ref, g_ref, keep_ref, dq_ref, dk_ref, dv_ref):
    keys_all, values_all = (k_ref[...], v_ref[...])
    keep = keep_ref[...] > 0
    sums = None
    for queries, grads, keys_part in zip(
        lane_parts(q_ref[...] * HD ** (-0.5)), lane_parts(g_ref[...]), lane_parts(keys_all)
    ):
        scores = contract_cols(keys_all, queries)
        scores = jnp.where(keep, scores, MASKED)
        weights = jnp.exp(scores - jnp.max(scores, axis=0, keepdims=True))
        weights = weights * (1.0 / jnp.sum(weights, axis=0, keepdims=True))
        grad_values = product(weights.astype(jnp.bfloat16), grads)
        grad_weights = contract_cols(values_all, grads)
        inner = jnp.sum(grad_weights * weights, axis=0, keepdims=True)
        grad_scores = (weights * (grad_weights - inner)).astype(jnp.bfloat16)
        grad_keys = product(grad_scores, queries)
        grad_queries = contract_rows(grad_scores, keys_part)
        parts = (grad_queries, grad_keys, grad_values)
        sums = parts if sums is None else tuple(a + b for a, b in zip(sums, parts))
    dq_ref[...] = (sums[0] * HD ** (-0.5)).astype(jnp.bfloat16)
    dk_ref[...] = sums[1].astype(jnp.bfloat16)
    dv_ref[...] = sums[2].astype(jnp.bfloat16)


def attend_back_group(stacked, grad_mixed, key_keep, group):
    length = stacked.shape[0]
    columns = [pl.BlockSpec((length, 128), group_block(2 * group, part)) for part in range(3)]
    result = pl.BlockSpec((length, 128), lambda j: (0, j))
    shape = jax.ShapeDtypeStruct((length, 256), jnp.bfloat16)
    parts = pl.pallas_call(
        attend_back_kernel,
        grid=(2,),
        in_specs=columns
        + [
            pl.BlockSpec((length, 128), lambda j: (0, 2 * group + j)),
            pl.BlockSpec((length, 1), lambda j: (0, 0)),
        ],
        out_specs=[result, result, result],
        out_shape=[shape, shape, shape],
        name="attend_back",
    )(stacked, stacked, stacked, grad_mixed, key_keep)
    return jnp.concatenate(parts, axis=1)


def own_image(
    tokens_in,
    cotangent,
    group_count,
    key_mask,
    ln1_gain,
    ln1_shift,
    w_query,
    b_query,
    w_key,
    w_value,
    b_value,
    w_out,
    b_out,
    ln2_gain,
    ln2_shift,
    w_up,
    b_up,
    w_down,
    b_down,
):
    low = jnp.bfloat16
    slot_count, tok_dev, width = tokens_in.shape
    core, place = (lax.axis_index("core"), lax.axis_index("z"))
    here_x, here_y = (lax.axis_index("x"), lax.axis_index("y"))
    depth = lax.axis_size("z")
    planes = 4
    length = depth * tok_dev
    block = width // (2 * planes)
    part_rows = w_query.shape[0]
    half = width // 2
    ff_half = w_up.shape[1] // 2
    ff_block = ff_half // planes
    ff_rows = w_down.shape[0]
    count = 8
    small_size = count * part_rows + b_up.shape[0]

    def to_image(local, *earlier):
        images = in_order(
            core, half_cols(core, local), swap_core(half_cols(1 - core, local)), 0
        ).reshape(2 * slot_count, tok_dev, half)
        mine = trade_z(after(images, *earlier)).reshape(length, half)
        return (side_by_side(core, mine, swap_core(mine)), mine)

    def to_tokens(mine, *earlier):
        parts = trade_z(after(mine.reshape(depth, tok_dev, half), *earlier))
        images = parts.reshape(2, slot_count, tok_dev, half)
        tokens = side_by_side(core, take(core, images), swap_core(take(1 - core, images)))
        return (tokens, parts)

    vectors = (ln1_gain, ln1_shift, b_query, b_value, b_out, ln2_gain, ln2_shift, b_down, b_up)
    small = jnp.concatenate(vectors).astype(low)
    small_rows = jnp.pad(small, (0, part_rows * 128 - small_size)).reshape(part_rows, 128)
    columns = [parity_cols(w, block) for w in (w_query, w_key, w_value)]
    ordered = [
        part
        for first in (0, 2, planes, planes + 2)
        for parts in columns
        for part in parts[first : first + 2]
    ]
    ordered = jnp.concatenate(ordered, axis=1).astype(low)
    project = gather_z(jnp.concatenate([ordered, small_rows], axis=1))

    up_local = jnp.concatenate([part.astype(low) for part in parity_cols(w_up, ff_block)], axis=1)
    up_pair = in_order(core, half_cols(core, up_local), swap_core(half_cols(1 - core, up_local)), 0)
    up_pair = up_pair.reshape(2 * part_rows, ff_half)
    shard = jnp.concatenate(
        [w_down.astype(low), up_pair[:, :width], up_pair[:, width:], w_out.astype(low)], axis=0
    )
    gathered = lax.all_gather(shard, ("y", "x", "z"), axis=0, tiled=False)

    image_in, _ = to_image(tokens_in, project)
    small_part = project[..., 6 * half :]
    project_pair = in_order(
        core,
        jnp.concatenate([half_cols(core, project[..., : 6 * half]), small_part], axis=-1),
        swap_core(
            jnp.concatenate([half_cols(1 - core, project[..., : 6 * half]), small_part], axis=-1)
        ),
        0,
    )
    project_all = gather_plane(project_pair.reshape(2 * depth * part_rows, 3 * half + 128))
    qkv_w = project_all[:, : 3 * half]
    small_all = project_all[:, 3 * half :].reshape(-1, part_rows * 128)[:, :small_size]
    small_all = small_all.astype(jnp.float32)
    wide = small_all[:, : count * part_rows].reshape(-1, count, part_rows)
    wide = wide.transpose(1, 0, 2).reshape(count, width)
    gain_one, shift_one, query_b, value_b, out_b, gain_two, shift_two, down_b = [
        wide[index] for index in range(count)
    ]

    def own_cols(vector, size):
        return jnp.where(
            core == 0,
            jnp.concatenate(parity_cols(vector, size)[:planes]),
            jnp.concatenate(parity_cols(vector, size)[planes:]),
        )

    query_b = own_cols(query_b, block)
    value_b = own_cols(value_b, block)
    up_b = own_cols(small_all[:, count * part_rows :].reshape(2 * ff_half), ff_block)

    live_slot = jnp.arange(slot_count) < group_count[0]
    live_low = live_slot.astype(low)[:, None, None]
    upstream_low, upstream_half = to_image(cotangent * live_low, image_in)

    owner, slot = (place // slot_count, place % slot_count)
    mask_mine = take(slot, key_mask).astype(jnp.float32)[None, :]
    key_keep = jnp.where(core == owner, mask_mine, swap_core(mask_mine))
    key_column = key_keep.reshape(length, 1)

    inputs = image_in.astype(jnp.float32)
    normal_one, inverse_one = norm_stats(inputs)
    normed_one = (normal_one * gain_one + shift_one).astype(low)
    group = half // 2
    none = jnp.zeros_like(query_b[:group])
    qkv_b = jnp.concatenate(
        [query_b[:group], none, value_b[:group], query_b[group:], none, value_b[group:]]
    )
    stacked = (product(normed_one, qkv_w) + qkv_b).astype(low)
    mixed = attend(stacked, key_keep)
    gathered = after(gathered, mixed)
    down_w = gathered[:, :ff_rows].reshape(ff_half, width)

    def by_feature(rows):
        return (
            rows.reshape(planes, depth, 2, part_rows, width)
            .transpose(0, 2, 1, 3, 4)
            .reshape(width, width)
        )

    up_w = jnp.concatenate(
        [
            by_feature(gathered[:, ff_rows : ff_rows + 2 * part_rows]),
            by_feature(gathered[:, ff_rows + 2 * part_rows : ff_rows + 4 * part_rows]),
        ],
        axis=1,
    )
    out_mine = gathered[:, ff_rows + 4 * part_rows :].reshape(half, width)
    out_other = swap_core(out_mine)
    mixed_other = swap_core(mixed)
    middle = inputs + (product(mixed, out_mine) + product(mixed_other, out_other)) + out_b
    normal_two, inverse_two = norm_stats(middle)
    normed_two = (normal_two * gain_two + shift_two).astype(low)
    hidden = product(normed_two, up_w) + up_b
    gate_sig = jax.nn.sigmoid(SLOPE * hidden)
    activated = (hidden * gate_sig).astype(low)
    grad_act = contract_cols(upstream_low, down_w)
    grad_hidden = (grad_act * (gate_sig + SLOPE * hidden * gate_sig * (1.0 - gate_sig))).astype(low)

    y_then_x = (along_y, here_y, swap_y)
    x_then_y = (along_x, here_x, swap_x)

    def begin(left, right):
        middle = right.shape[1] // 2
        first, first_sent = scatter_start(*y_then_x, left, right[:, :middle])
        second, second_sent = scatter_start(*x_then_y, left, right[:, middle:])
        return (left, right, first, second, first_sent, second_sent)

    def proceed(state, *earlier):
        left, right, first, second = state[:4]
        first, second = lax.optimization_barrier((first, second) + earlier)[:2]
        middle = right.shape[1] // 2
        first = scatter_next(along_y, here_y, here_x, swap_x, left, right[:, :middle], first)
        second = scatter_next(along_x, here_x, here_y, swap_y, left, right[:, middle:], second)
        return first + second

    def finish(state, *earlier):
        first_kept, first_got, _, second_kept, second_got, _ = state
        first_got, second_got = lax.optimization_barrier((first_got, second_got) + earlier)[:2]
        return (first_kept + first_got, second_kept + second_got)

    down_state = begin(activated, upstream_low)
    grad_two = contract_cols(after(grad_hidden, *down_state[4:]), up_w)
    grad_two_other = swap_core(grad_two)
    up_state = begin(normed_two, after(grad_hidden, grad_two))
    grad_normed_two = grad_two + after(grad_two_other, *up_state[4:])

    upstream = upstream_low.astype(jnp.float32)
    grad_mid, grad_gain_two, grad_shift_two = norm_back(
        grad_normed_two, normal_two, inverse_two, gain_two
    )
    grad_middle = upstream + grad_mid
    branch_low = grad_middle.astype(low)
    grad_mixed = contract_cols(branch_low, out_mine).astype(low)

    result = product(after(activated, grad_two), down_w)
    result = half_cols(core, middle + down_b) + (
        half_cols(core, result) + swap_core(half_cols(1 - core, result))
    )
    block_tokens, block_parts = to_tokens(result.astype(low))
    block_out = block_tokens * live_low

    out_state = begin(mixed, branch_low)
    down_state = proceed(down_state, grad_mixed)
    grad_mixed = after(grad_mixed, *out_state[4:], down_state[2], down_state[5])
    grad_first_group = attend_back_group(stacked, grad_mixed, key_column, 0)
    up_state = proceed(up_state, grad_first_group)
    first_group, first_sent = scatter_start(*y_then_x, normed_one, grad_first_group)
    grad_mixed = after(grad_mixed, up_state[2], up_state[5], first_sent)
    grad_second_group = attend_back_group(stacked, grad_mixed, key_column, 1)
    down_first, down_second = finish(down_state, grad_first_group)
    down_parts = trade_z(
        after(
            jnp.concatenate([down_first, down_second], axis=1)
            .reshape(depth, ff_rows, width)
            .astype(low),
            block_parts,
        )
    )
    out_state = proceed(out_state, grad_first_group)
    second_group, second_sent = scatter_start(*x_then_y, normed_one, grad_second_group)
    grad_qkv = jnp.concatenate([grad_first_group, grad_second_group], axis=1)

    grad_one = contract_cols(after(grad_qkv, second_sent), qkv_w)
    scaled = grad_one * gain_one
    sums = jnp.concatenate(
        [
            jnp.sum(scaled, axis=1, keepdims=True),
            jnp.sum(scaled * normal_one, axis=1, keepdims=True),
        ],
        axis=1,
    )
    got = swap_core(
        jnp.concatenate(
            [half_cols(1 - core, grad_one), jnp.pad(sums, ((0, 0), (0, 126)))], axis=1
        )
    )

    up_first, up_second = finish(up_state, grad_second_group)
    out_first, out_second = finish(out_state, grad_second_group)

    def by_place(rows):
        return rows.reshape(2, depth, part_rows, -1).transpose(1, 0, 2, 3)

    wide_parts = trade_z(
        after(
            jnp.concatenate(
                [
                    by_place(up_first).reshape(depth, 2 * part_rows, width),
                    by_place(up_second).reshape(depth, 2 * part_rows, width),
                    jnp.concatenate([out_first, out_second], axis=1).reshape(
                        depth, part_rows, width
                    ),
                ],
                axis=1,
            ).astype(low),
            down_parts,
        )
    )

    grad_normed_one = half_cols(core, grad_one) + got[:, :half]
    means = (sums + got[:, half : half + 2]) / width
    normal_mine = half_cols(core, normal_one)
    grad_first = inverse_one * (
        grad_normed_one * half_cols(core, gain_one) - means[:, :1] - normal_mine * means[:, 1:]
    )
    input_grad, input_parts = to_tokens(
        (half_cols(core, grad_middle) + grad_first).astype(low), wide_parts
    )

    first_group = scatter_next(
        along_y, here_y, here_x, swap_x, normed_one, grad_first_group, after(first_group, grad_one)
    )
    second_group = scatter_next(
        along_x, here_x, here_y, swap_y, normed_one, grad_second_group, after(second_group, grad_one)
    )
    project_first, project_second = finish(first_group + second_group)

    bias_qkv = jnp.sum(grad_qkv.astype(jnp.float32), axis=0)

    def placed(mine):
        none = jnp.zeros_like(mine)
        return side_by_side(core, mine, none)

    bias_parts = jnp.stack(
        [
            jnp.concatenate([bias_qkv[:group], bias_qkv[3 * group : 4 * group]]),
            jnp.concatenate([bias_qkv[2 * group : 3 * group], bias_qkv[5 * group :]]),
        ]
    ).reshape(2, planes, block)
    bias_parts = in_order(core, bias_parts, jnp.zeros_like(bias_parts), 2).reshape(2, width)
    first_core = (core == 0).astype(jnp.float32)
    small_grads = jnp.stack(
        [
            jnp.sum(grad_one * normal_one, axis=0),
            jnp.sum(grad_one, axis=0),
            bias_parts[0],
            bias_parts[1],
            first_core * jnp.sum(branch_low.astype(jnp.float32), axis=0),
            first_core * grad_gain_two,
            first_core * grad_shift_two,
            placed(jnp.sum(upstream_half.astype(jnp.float32), axis=0)),
        ]
    )
    small_wide = small_grads.reshape(count, 2 * planes * depth, part_rows)
    small_wide = small_wide.transpose(1, 0, 2).reshape(planes, 2, depth, count * part_rows)
    grad_up_b = jnp.sum(grad_hidden.astype(jnp.float32), axis=0).reshape(planes, depth, -1)
    grad_up_b = in_order(core, grad_up_b, jnp.zeros_like(grad_up_b), 1)
    small_wide = jnp.concatenate([small_wide, grad_up_b], axis=-1).reshape(2, 2, -1)
    small_sum = take(here_y, small_wide) + swap_y(take(1 - here_y, small_wide))
    small_sum = take(here_x, small_sum) + swap_x(take(1 - here_x, small_sum))
    small_sum = small_sum.reshape(2, depth, small_size).transpose(1, 0, 2)
    small_sum = jnp.pad(small_sum, ((0, 0), (0, 0), (0, part_rows * 128 - small_size)))
    small_sum = small_sum.reshape(depth, 2, part_rows, 128)

    down_rows = jnp.sum(down_parts.astype(jnp.float32), axis=0)
    wide_parts = jnp.sum(wide_parts.astype(jnp.float32), axis=0)
    out_rows = wide_parts[4 * part_rows :]
    up_pair = jnp.concatenate(
        [wide_parts[: 2 * part_rows], wide_parts[2 * part_rows : 4 * part_rows]], axis=1
    ).reshape(2, part_rows, ff_half)
    mine, other = (take(core, up_pair), swap_core(take(1 - core, up_pair)))
    up_rows = natural_cols(
        jnp.where(core == 0, mine, other), jnp.where(core == 0, other, mine), ff_block
    )

    project_parts = jnp.concatenate(
        [by_place(project_first), by_place(project_second), small_sum], axis=-1
    ).astype(low)
    project_pair = jnp.sum(trade_z(after(project_parts, input_parts)).astype(jnp.float32), axis=0)
    mine, other = (take(core, project_pair), swap_core(take(1 - core, project_pair)))
    even = jnp.where(core == 0, mine, other)
    odd = jnp.where(core == 0, other, mine)

    def member(value, index):
        return jnp.concatenate(
            [value[:, k * group : (k + 1) * group] for k in (index, index + 3)], axis=1
        )

    query_rows, key_rows, value_rows = [
        natural_cols(member(even, k), member(odd, k), block) for k in range(3)
    ]
    small_out = (mine[:, 3 * half :] + other[:, 3 * half :]).reshape(-1)
    pieces = [small_out[k * part_rows : (k + 1) * part_rows] for k in range(count)]
    return (
        block_out,
        input_grad,
        pieces[0],
        pieces[1],
        query_rows,
        pieces[2],
        key_rows,
        value_rows,
        pieces[3],
        out_rows,
        pieces[4],
        pieces[5],
        pieces[6],
        up_rows,
        small_out[count * part_rows : small_size],
        down_rows,
        pieces[7],
    )


def named_image(*args):
    return own_image(*args)


def solution(mesh):
    dp, seq = (mesh.shape["dp"], mesh.shape["seq"])
    function, axes, by_image, by_part = (per_device, mesh, "dp", ("dp", "seq"))
    by_token = "seq"
    if dp == 8 and seq == 4:
        function = named_image
        axes = jax.sharding.Mesh(mesh.devices.reshape(2, 2, 2, seq), ("y", "x", "core", "z"))
        by_image, by_token = (("y", "x", "core"), "z")
        by_part = ("y", "x", "core", "z")
    tokens, vector, matrix = (P(by_image, by_token, None), P(by_part), P(by_part, None))
    params = (
        (vector, vector, matrix, vector, matrix, matrix, vector, matrix)
        + (vector, vector, vector, matrix, vector, matrix, vector)
    )
    return jax.shard_map(
        function,
        mesh=axes,
        in_specs=(tokens, tokens, P(by_image), P(by_image, None)) + params,
        out_specs=(tokens, tokens) + params,
        check_vma=False,
    )
```

```python
import jax
import jax.numpy as jnp
from jax import lax
from jax.experimental import pallas as pl
from jax.experimental.pallas import tpu as pltpu
from jax.sharding import PartitionSpec as P


HD = 64


EPSILON = 1e-05
SLOPE = 1.702
MASKED = -1000000000.0


def norm_stats(values):
    center = values - jnp.mean(values, axis=-1, keepdims=True)
    inverse = lax.rsqrt(jnp.mean(center * center, axis=-1, keepdims=True) + EPSILON)
    return (center * inverse, inverse)


def norm_back(incoming, normal, inverse, gain):
    scaled = incoming * gain
    rows_grad = inverse * (
        scaled
        - jnp.mean(scaled, axis=-1, keepdims=True)
        - normal * jnp.mean(scaled * normal, axis=-1, keepdims=True)
    )
    return (rows_grad, jnp.sum(incoming * normal, axis=0), jnp.sum(incoming, axis=0))


def product(left, right):
    return jnp.dot(left, right, preferred_element_type=jnp.float32)


def contract_rows(left, right):
    return lax.dot_general(
        left, right, (((0,), (0,)), ((), ())), preferred_element_type=jnp.float32
    )


def contract_cols(left, right):
    return lax.dot_general(
        left, right, (((1,), (1,)), ((), ())), preferred_element_type=jnp.float32
    )


def split_heads(stacked):
    length = stacked.shape[0]
    heads_here = stacked.shape[2] // HD
    queries = stacked[:, 0].reshape(length, heads_here, HD)
    keys_all = stacked[:, 1].reshape(length, heads_here, HD)
    values_all = stacked[:, 2].reshape(length, heads_here, HD)
    return (queries, keys_all, values_all)


def masked_scores(queries, keys_all, key_keep):
    scores = jnp.einsum(
        "qhd,khd->hqk", queries, keys_all, preferred_element_type=jnp.float32
    ) * HD ** (-0.5)
    return jnp.where(key_keep[None, None, :] > 0, scores, MASKED)


def attend_image(paired):
    stacked, key_keep = paired
    queries, keys_all, values_all = split_heads(stacked)
    scores = masked_scores(queries, keys_all, key_keep)
    row_peak = jnp.max(scores, axis=-1, keepdims=True)
    weights_exp = jnp.exp(scores - row_peak)
    row_total = jnp.sum(weights_exp, axis=-1, keepdims=True)
    weights_soft = weights_exp / row_total
    mixed_out = jnp.einsum(
        "hqk,khd->qhd",
        weights_soft.astype(jnp.bfloat16),
        values_all,
        preferred_element_type=jnp.float32,
    )
    log_total = (row_peak + jnp.log(row_total))[..., 0]
    return (mixed_out.reshape(stacked.shape[0], stacked.shape[2]).astype(jnp.bfloat16), log_total)


def attend_back(packed):
    stacked, grad_mixed, log_total, key_keep = packed
    queries, keys_all, values_all = split_heads(stacked)
    scores = masked_scores(queries, keys_all, key_keep)
    weights_soft = jnp.exp(scores - log_total[..., None])
    grad_mix = grad_mixed.reshape(queries.shape)
    grad_values = jnp.einsum(
        "hqk,qhd->khd",
        weights_soft.astype(jnp.bfloat16),
        grad_mix,
        preferred_element_type=jnp.float32,
    )
    grad_weights = jnp.einsum(
        "qhd,khd->hqk", grad_mix, values_all, preferred_element_type=jnp.float32
    )
    row_inner = jnp.sum(grad_weights * weights_soft, axis=-1, keepdims=True)
    grad_scores = (weights_soft * (grad_weights - row_inner)).astype(jnp.bfloat16)
    grad_queries = jnp.einsum(
        "hqk,khd->qhd", grad_scores, keys_all, preferred_element_type=jnp.float32
    ) * HD ** (-0.5)
    grad_keys = jnp.einsum(
        "hqk,qhd->khd", grad_scores, queries, preferred_element_type=jnp.float32
    ) * HD ** (-0.5)
    length = stacked.shape[0]
    return jnp.stack(
        [
            grad_queries.reshape(length, -1),
            grad_keys.reshape(length, -1),
            grad_values.reshape(length, -1),
        ],
        axis=1,
    ).astype(jnp.bfloat16)


def per_device(
    tokens_in,
    cotangent,
    group_count,
    key_mask,
    ln1_gain,
    ln1_shift,
    w_query,
    b_query,
    w_key,
    w_value,
    b_value,
    w_out,
    b_out,
    ln2_gain,
    ln2_shift,
    w_up,
    b_up,
    w_down,
    b_down,
):
    slot_count, tok_dev, width = tokens_in.shape
    row_count = slot_count * tok_dev
    shared = (
        lax.all_gather(ln1_gain.astype(jnp.bfloat16), ("dp", "seq"), axis=0, tiled=True),
        lax.all_gather(ln1_shift.astype(jnp.bfloat16), ("dp", "seq"), axis=0, tiled=True),
        lax.all_gather(w_query.astype(jnp.bfloat16), ("dp", "seq"), axis=0, tiled=True),
        lax.all_gather(b_query.astype(jnp.bfloat16), ("dp", "seq"), axis=0, tiled=True),
        lax.all_gather(w_key.astype(jnp.bfloat16), ("dp", "seq"), axis=0, tiled=True),
        lax.all_gather(w_value.astype(jnp.bfloat16), ("dp", "seq"), axis=0, tiled=True),
        lax.all_gather(b_value.astype(jnp.bfloat16), ("dp", "seq"), axis=0, tiled=True),
        lax.all_gather(w_out.astype(jnp.bfloat16), ("dp", "seq"), axis=0, tiled=True),
        lax.all_gather(b_out.astype(jnp.bfloat16), ("dp", "seq"), axis=0, tiled=True),
        lax.all_gather(ln2_gain.astype(jnp.bfloat16), ("dp", "seq"), axis=0, tiled=True),
        lax.all_gather(ln2_shift.astype(jnp.bfloat16), ("dp", "seq"), axis=0, tiled=True),
        lax.all_gather(w_up.astype(jnp.bfloat16), ("dp", "seq"), axis=0, tiled=True),
        lax.all_gather(b_up.astype(jnp.bfloat16), ("dp", "seq"), axis=0, tiled=True),
        lax.all_gather(w_down.astype(jnp.bfloat16), ("dp", "seq"), axis=0, tiled=True),
        lax.all_gather(b_down.astype(jnp.bfloat16), ("dp", "seq"), axis=0, tiled=True),
    )
    (
        gain_one,
        shift_one,
        query_w,
        query_b,
        key_w,
        value_w,
        value_b,
        out_w,
        out_b,
        gain_two,
        shift_two,
        up_w,
        up_b,
        down_w,
        down_b,
    ) = shared
    live_slot = (jnp.arange(slot_count) < group_count[0]).astype(jnp.float32)[:, None, None]
    inputs = tokens_in.astype(jnp.float32).reshape(row_count, width)
    normal_one, inverse_one = norm_stats(inputs)
    normed_one = (normal_one * gain_one + shift_one).astype(jnp.bfloat16)
    queries = (product(normed_one, query_w) + query_b).astype(jnp.bfloat16)
    keys_all = product(normed_one, key_w).astype(jnp.bfloat16)
    values_all = (product(normed_one, value_w) + value_b).astype(jnp.bfloat16)
    stacked = jnp.stack([queries, keys_all, values_all], axis=1).reshape(
        slot_count, tok_dev, 3, width
    )
    by_heads = lax.all_to_all(stacked, "seq", split_axis=3, concat_axis=1, tiled=True)
    mixed_heads, log_total = lax.map(attend_image, (by_heads, key_mask))
    mixed_tok = lax.all_to_all(mixed_heads, "seq", split_axis=1, concat_axis=2, tiled=True).reshape(
        row_count, width
    )
    middle = inputs + product(mixed_tok, out_w) + out_b
    normal_two, inverse_two = norm_stats(middle)
    normed_two = (normal_two * gain_two + shift_two).astype(jnp.bfloat16)
    hidden = product(normed_two, up_w) + up_b
    gate_sig = jax.nn.sigmoid(SLOPE * hidden)
    activated = (hidden * gate_sig).astype(jnp.bfloat16)
    result = middle + product(activated, down_w) + down_b
    block_out = (result.reshape(slot_count, tok_dev, width) * live_slot).astype(jnp.bfloat16)
    upstream = (cotangent.astype(jnp.float32) * live_slot).reshape(row_count, width)
    upstream_low = upstream.astype(jnp.bfloat16)
    grad_down = contract_rows(activated, upstream_low)
    grad_down_b = jnp.sum(upstream, axis=0)
    grad_act = contract_cols(upstream_low, down_w)
    grad_hidden = (grad_act * (gate_sig + SLOPE * hidden * gate_sig * (1.0 - gate_sig))).astype(
        jnp.bfloat16
    )
    grad_up = contract_rows(normed_two, grad_hidden)
    grad_up_b = jnp.sum(grad_hidden.astype(jnp.float32), axis=0)
    grad_normed_two = contract_cols(grad_hidden, up_w)
    grad_mid, grad_gain_two, grad_shift_two = norm_back(
        grad_normed_two, normal_two, inverse_two, gain_two
    )
    grad_middle = upstream + grad_mid
    branch_low = grad_middle.astype(jnp.bfloat16)
    grad_out = contract_rows(mixed_tok, branch_low)
    grad_out_b = jnp.sum(branch_low.astype(jnp.float32), axis=0)
    grad_mixed = (
        contract_cols(branch_low, out_w).astype(jnp.bfloat16).reshape(slot_count, tok_dev, width)
    )
    grad_by_heads = lax.all_to_all(grad_mixed, "seq", split_axis=2, concat_axis=1, tiled=True)
    grad_stacked = lax.map(attend_back, (by_heads, grad_by_heads, log_total, key_mask))
    grad_tok = lax.all_to_all(grad_stacked, "seq", split_axis=1, concat_axis=3, tiled=True).reshape(
        row_count, 3, width
    )
    grad_q_rows = grad_tok[:, 0]
    grad_k_rows = grad_tok[:, 1]
    grad_v_rows = grad_tok[:, 2]
    grad_query = contract_rows(normed_one, grad_q_rows)
    grad_query_b = jnp.sum(grad_q_rows.astype(jnp.float32), axis=0)
    grad_key = contract_rows(normed_one, grad_k_rows)
    grad_value = contract_rows(normed_one, grad_v_rows)
    grad_value_b = jnp.sum(grad_v_rows.astype(jnp.float32), axis=0)
    grad_normed_one = (
        contract_cols(grad_q_rows, query_w)
        + contract_cols(grad_k_rows, key_w)
        + contract_cols(grad_v_rows, value_w)
    )
    grad_first, grad_gain_one, grad_shift_one = norm_back(
        grad_normed_one, normal_one, inverse_one, gain_one
    )
    input_grad = (grad_middle + grad_first).astype(jnp.bfloat16).reshape(slot_count, tok_dev, width)
    every_shard = (
        lax.psum_scatter(grad_gain_one, ("dp", "seq"), scatter_dimension=0, tiled=True),
        lax.psum_scatter(grad_shift_one, ("dp", "seq"), scatter_dimension=0, tiled=True),
        lax.psum_scatter(grad_query, ("dp", "seq"), scatter_dimension=0, tiled=True),
        lax.psum_scatter(grad_query_b, ("dp", "seq"), scatter_dimension=0, tiled=True),
        lax.psum_scatter(grad_key, ("dp", "seq"), scatter_dimension=0, tiled=True),
        lax.psum_scatter(grad_value, ("dp", "seq"), scatter_dimension=0, tiled=True),
        lax.psum_scatter(grad_value_b, ("dp", "seq"), scatter_dimension=0, tiled=True),
        lax.psum_scatter(grad_out, ("dp", "seq"), scatter_dimension=0, tiled=True),
        lax.psum_scatter(grad_out_b, ("dp", "seq"), scatter_dimension=0, tiled=True),
        lax.psum_scatter(grad_gain_two, ("dp", "seq"), scatter_dimension=0, tiled=True),
        lax.psum_scatter(grad_shift_two, ("dp", "seq"), scatter_dimension=0, tiled=True),
        lax.psum_scatter(grad_up, ("dp", "seq"), scatter_dimension=0, tiled=True),
        lax.psum_scatter(grad_up_b, ("dp", "seq"), scatter_dimension=0, tiled=True),
        lax.psum_scatter(grad_down, ("dp", "seq"), scatter_dimension=0, tiled=True),
        lax.psum_scatter(grad_down_b, ("dp", "seq"), scatter_dimension=0, tiled=True),
    )
    return (block_out, input_grad) + tuple(every_shard)


def swap_core(value):
    return lax.ppermute(value, "core", [(0, 1), (1, 0)])


def swap_x(value):
    return lax.ppermute(value, "x", [(0, 1), (1, 0)])


def swap_y(value):
    return lax.ppermute(value, "y", [(0, 1), (1, 0)])


def trade_z(value):
    return lax.all_to_all(value, "z", split_axis=0, concat_axis=0, tiled=True)


def in_order(index, mine, other, axis):
    return jnp.where(
        index == 0, jnp.stack([mine, other], axis=axis), jnp.stack([other, mine], axis=axis)
    )


def side_by_side(index, mine, other):
    return jnp.where(
        index == 0,
        jnp.concatenate([mine, other], axis=-1),
        jnp.concatenate([other, mine], axis=-1),
    )


def half_cols(index, value):
    middle = value.shape[-1] // 2
    return jnp.where(index == 0, value[..., :middle], value[..., middle:])


def take(index, value):
    return lax.dynamic_index_in_dim(value, index, 0, keepdims=False)


def after(value, *earlier):
    return lax.optimization_barrier((value,) + earlier)[0]


def parity_cols(value, size):
    count = value.shape[-1] // size
    parts = [value[..., k * size : (k + 1) * size] for k in range(count)]
    return parts[0::2] + parts[1::2]


def natural_cols(even, odd, size):
    parts = []
    for k in range(even.shape[-1] // size):
        parts += [even[..., k * size : (k + 1) * size], odd[..., k * size : (k + 1) * size]]
    return jnp.concatenate(parts, axis=-1)


def gather_z(shard):
    copies = lax.axis_size("z")
    return trade_z(jnp.broadcast_to(shard[None], (copies,) + shard.shape))


def gather_plane(rows):
    here_x, here_y = (lax.axis_index("x"), lax.axis_index("y"))
    half = rows.shape[0] // 2
    first, second = (rows[:half], rows[half:])
    first_x = swap_x(first)
    second_y = swap_y(second)
    first_pair = in_order(here_x, first, first_x, 0)
    second_pair = in_order(here_y, second, second_y, 0)
    first_y = swap_y(first_pair)
    second_x = swap_x(second_pair)
    first_all = in_order(here_y, first_pair, first_y, 0)
    second_all = in_order(here_x, second_pair, second_x, 1)
    return jnp.stack([first_all, second_all], axis=2).reshape(4 * rows.shape[0], rows.shape[1])


def along_y(index, value):
    return half_cols(index, value)


def along_x(index, value):
    middle = value.shape[1] // 2
    return jnp.concatenate(
        [half_cols(index, value[:, :middle]), half_cols(index, value[:, middle:])], axis=1
    )


def scatter_start(pick, index, swap, left, right):
    sent = contract_rows(pick(1 - index, left), right).astype(jnp.bfloat16)
    return (swap(sent), sent)


def scatter_next(pick, index, next_index, swap, left, right, got):
    total = contract_rows(pick(index, left), right) + got
    total = total.reshape(2, total.shape[0] // 2, total.shape[1])
    sent = take(1 - next_index, total).astype(jnp.bfloat16)
    return (take(next_index, total), swap(sent), sent)


def add_up(parts):
    return jnp.sum(parts.astype(jnp.float32), axis=0)


VMEM_LIMIT = 20 * 2**20


def lane_parts(value):
    lane = lax.broadcasted_iota(jnp.int32, value.shape, 1)
    none = jnp.zeros_like(value)
    return (jnp.where(lane < HD, value, none), jnp.where(lane < HD, none, value))


def attend_kernel(q_ref, k_ref, v_ref, keep_ref, out_ref):
    keys_all = k_ref[...]
    keep = keep_ref[...] > 0
    total = None
    for queries, values in zip(lane_parts(q_ref[...] * HD ** (-0.5)), lane_parts(v_ref[...])):
        scores = contract_cols(queries, keys_all)
        scores = jnp.where(keep, scores, MASKED)
        weights = jnp.exp(scores - jnp.max(scores, axis=1, keepdims=True))
        weights = weights * (1.0 / jnp.sum(weights, axis=1, keepdims=True))
        part = product(weights.astype(jnp.bfloat16), values)
        total = part if total is None else total + part
    out_ref[...] = total.astype(jnp.bfloat16)


def group_block(first, part):
    return lambda j: (0, (first + j) // 2 * 6 + 2 * part + (first + j) % 2)


def attend(stacked, key_keep):
    length, pairs = (stacked.shape[0], stacked.shape[1] // 384)
    columns = [pl.BlockSpec((length, 128), group_block(0, part)) for part in range(3)]
    return pl.pallas_call(
        attend_kernel,
        grid=(pairs,),
        in_specs=columns + [pl.BlockSpec((1, length), lambda j: (0, 0))],
        out_specs=pl.BlockSpec((length, 128), lambda j: (0, j)),
        out_shape=jax.ShapeDtypeStruct((length, pairs * 128), jnp.bfloat16),
        compiler_params=pltpu.CompilerParams(vmem_limit_bytes=VMEM_LIMIT),
        name="attend",
    )(stacked, stacked, stacked, key_keep)


def attend_back_kernel(q_ref, k_ref, v_ref, g_ref, keep_ref, out_ref):
    keys_all, values_all = (k_ref[...], v_ref[...])
    keep = keep_ref[...] > 0
    sums = None
    for queries, grads, keys_part in zip(
        lane_parts(q_ref[...] * HD ** (-0.5)), lane_parts(g_ref[...]), lane_parts(keys_all)
    ):
        scores = contract_cols(keys_all, queries)
        scores = jnp.where(keep, scores, MASKED)
        weights = jnp.exp(scores - jnp.max(scores, axis=0, keepdims=True))
        weights = weights * (1.0 / jnp.sum(weights, axis=0, keepdims=True))
        grad_values = product(weights.astype(jnp.bfloat16), grads)
        grad_weights = contract_cols(values_all, grads)
        inner = jnp.sum(grad_weights * weights, axis=0, keepdims=True)
        grad_scores = (weights * (grad_weights - inner)).astype(jnp.bfloat16)
        grad_keys = product(grad_scores, queries)
        grad_queries = contract_rows(grad_scores, keys_part)
        parts = (grad_queries, grad_keys, grad_values)
        sums = parts if sums is None else tuple(a + b for a, b in zip(sums, parts))
    sums = (sums[0] * HD ** (-0.5), sums[1], sums[2])
    for pair in range(2):

        @pl.when(pl.program_id(0) == pair)
        def _():
            for part in range(3):
                start = part * 256 + pair * 128
                out_ref[:, start : start + 128] = sums[part].astype(jnp.bfloat16)


def attend_back_group(stacked, grad_mixed, key_keep, group):
    length = stacked.shape[0]
    columns = [pl.BlockSpec((length, 128), group_block(2 * group, part)) for part in range(3)]
    return pl.pallas_call(
        attend_back_kernel,
        grid=(2,),
        in_specs=columns
        + [
            pl.BlockSpec((length, 128), lambda j: (0, 2 * group + j)),
            pl.BlockSpec((length, 1), lambda j: (0, 0)),
        ],
        out_specs=pl.BlockSpec((length, 768), lambda j: (0, 0)),
        out_shape=jax.ShapeDtypeStruct((length, 768), jnp.bfloat16),
        compiler_params=pltpu.CompilerParams(vmem_limit_bytes=VMEM_LIMIT),
        name="attend_back",
    )(stacked, stacked, stacked, grad_mixed, key_keep)


def own_image(
    tokens_in,
    cotangent,
    group_count,
    key_mask,
    ln1_gain,
    ln1_shift,
    w_query,
    b_query,
    w_key,
    w_value,
    b_value,
    w_out,
    b_out,
    ln2_gain,
    ln2_shift,
    w_up,
    b_up,
    w_down,
    b_down,
):
    low = jnp.bfloat16
    slot_count, tok_dev, width = tokens_in.shape
    core, place = (lax.axis_index("core"), lax.axis_index("z"))
    here_x, here_y = (lax.axis_index("x"), lax.axis_index("y"))
    depth = lax.axis_size("z")
    planes = 4
    length = depth * tok_dev
    block = width // (2 * planes)
    part_rows = w_query.shape[0]
    half = width // 2
    ff_half = w_up.shape[1] // 2
    ff_block = ff_half // planes
    ff_rows = w_down.shape[0]
    count = 8
    small_size = count * part_rows + b_up.shape[0]

    def to_image(local, *earlier):
        images = in_order(
            core, half_cols(core, local), swap_core(half_cols(1 - core, local)), 0
        ).reshape(2 * slot_count, tok_dev, half)
        mine = trade_z(after(images, *earlier)).reshape(length, half)
        return (side_by_side(core, mine, swap_core(mine)), mine)

    def to_tokens(mine, *earlier):
        parts = trade_z(after(mine.reshape(depth, tok_dev, half), *earlier))
        images = parts.reshape(2, slot_count, tok_dev, half)
        tokens = side_by_side(core, take(core, images), swap_core(take(1 - core, images)))
        return (tokens, parts)

    vectors = (ln1_gain, ln1_shift, b_query, b_value, b_out, ln2_gain, ln2_shift, b_down, b_up)
    small = jnp.concatenate(vectors).astype(low)
    small_rows = jnp.pad(small, (0, part_rows * 128 - small_size)).reshape(part_rows, 128)
    columns = [parity_cols(w, block) for w in (w_query, w_key, w_value)]
    ordered = [
        part
        for first in (0, 2, planes, planes + 2)
        for parts in columns
        for part in parts[first : first + 2]
    ]
    ordered = jnp.concatenate(ordered, axis=1).astype(low)

    up_local = jnp.concatenate([part.astype(low) for part in parity_cols(w_up, ff_block)], axis=1)
    up_pair = in_order(core, half_cols(core, up_local), swap_core(half_cols(1 - core, up_local)), 0)
    up_pair = up_pair.reshape(2 * part_rows, ff_half)
    shard = jnp.concatenate(
        [w_down.astype(low), up_pair[:, :width], up_pair[:, width:], w_out.astype(low)], axis=0
    )
    gathered = lax.all_gather(shard, ("y", "x", "z"), axis=0, tiled=False)
    project = gather_z(after(jnp.concatenate([ordered, small_rows], axis=1), shard))

    image_in, token_half = to_image(tokens_in, project)
    small_part = project[..., 6 * half :]
    project_pair = in_order(
        core,
        jnp.concatenate([half_cols(core, project[..., : 6 * half]), small_part], axis=-1),
        swap_core(
            jnp.concatenate([half_cols(1 - core, project[..., : 6 * half]), small_part], axis=-1)
        ),
        0,
    )
    project_all = gather_plane(
        project_pair.reshape(2 * depth * part_rows, 3 * half + 128))
    qkv_w = project_all[:, : 3 * half]
    small_all = project_all[:, 3 * half :].reshape(-1, part_rows * 128)[:, :small_size]
    small_all = small_all.astype(jnp.float32)
    wide = small_all[:, : count * part_rows].reshape(-1, count, part_rows)
    wide = wide.transpose(1, 0, 2).reshape(count, width)
    gain_one, shift_one, query_b, value_b, out_b, gain_two, shift_two, down_b = [
        wide[index] for index in range(count)
    ]

    def own_cols(vector, size):
        return jnp.where(
            core == 0,
            jnp.concatenate(parity_cols(vector, size)[:planes]),
            jnp.concatenate(parity_cols(vector, size)[planes:]),
        )

    query_b = own_cols(query_b, block)
    value_b = own_cols(value_b, block)
    up_b = own_cols(small_all[:, count * part_rows :].reshape(2 * ff_half), ff_block)

    live_slot = jnp.arange(slot_count) < group_count[0]
    live_low = live_slot.astype(low)[:, None, None]
    upstream_low, upstream_half = to_image(cotangent * live_low, token_half)

    owner, slot = (place // slot_count, place % slot_count)
    mask_mine = take(slot, key_mask).astype(jnp.float32)[None, :]
    key_keep = jnp.where(core == owner, mask_mine, swap_core(mask_mine))
    key_column = key_keep.reshape(length, 1)

    inputs = image_in.astype(jnp.float32)
    normal_one, inverse_one = norm_stats(inputs)
    normed_one = (normal_one * gain_one + shift_one).astype(low)
    group = half // 2
    qkv_b = jnp.stack([query_b, jnp.zeros_like(query_b), value_b])
    qkv_b = qkv_b.reshape(3, 2, group).transpose(1, 0, 2).reshape(3 * half)
    stacked = (product(normed_one, qkv_w) + qkv_b).astype(low)
    mixed = attend(stacked, key_keep)
    gathered = after(gathered, mixed)

    def by_feature(rows):
        return (
            rows.reshape(planes, depth, 2, part_rows, width)
            .transpose(0, 2, 1, 3, 4)
            .reshape(width, width)
        )

    up_w = jnp.concatenate(
        [
            by_feature(gathered[:, ff_rows : ff_rows + 2 * part_rows]),
            by_feature(gathered[:, ff_rows + 2 * part_rows : ff_rows + 4 * part_rows]),
        ],
        axis=1,
    )
    out_mine = gathered[:, ff_rows + 4 * part_rows :].reshape(half, width)
    out_other = swap_core(out_mine)
    mixed_other = swap_core(mixed)
    down_w = gathered[:, :ff_rows].reshape(ff_half, width)
    middle = inputs + (product(mixed, out_mine) + product(mixed_other, out_other)) + out_b
    normal_two, inverse_two = norm_stats(middle)
    normed_two = (normal_two * gain_two + shift_two).astype(low)
    hidden = product(normed_two, up_w) + up_b
    gate_sig = jax.nn.sigmoid(SLOPE * hidden)
    activated = (hidden * gate_sig).astype(low)
    grad_act = contract_cols(upstream_low, down_w)
    grad_hidden = (grad_act * (gate_sig + SLOPE * hidden * gate_sig * (1.0 - gate_sig))).astype(low)

    y_then_x = (along_y, here_y, swap_y)
    x_then_y = (along_x, here_x, swap_x)

    def begin(left, right):
        middle = right.shape[1] // 2
        first, first_sent = scatter_start(*y_then_x, left, right[:, :middle])
        second, second_sent = scatter_start(*x_then_y, left, right[:, middle:])
        return (left, right, first, second, first_sent, second_sent)

    def proceed(state, *earlier):
        left, right, first, second = state[:4]
        left, right, first, second = lax.optimization_barrier(
            (left, right, first, second) + earlier
        )[:4]
        middle = right.shape[1] // 2
        first = scatter_next(along_y, here_y, here_x, swap_x, left, right[:, :middle], first)
        second = scatter_next(along_x, here_x, here_y, swap_y, left, right[:, middle:], second)
        return first + second

    def finish(state, *earlier):
        first_kept, first_got, _, second_kept, second_got, _ = state
        first_got, second_got = lax.optimization_barrier((first_got, second_got) + earlier)[:2]
        return (first_kept + first_got, second_kept + second_got)

    down_state = begin(activated, upstream_low)
    grad_two = contract_cols(after(grad_hidden, *down_state[4:]), up_w)
    grad_two_other = swap_core(grad_two)
    up_state = begin(normed_two, after(grad_hidden, grad_two))
    grad_normed_two = grad_two + after(grad_two_other, *up_state[4:])

    upstream = upstream_low.astype(jnp.float32)
    grad_mid, grad_gain_two, grad_shift_two = norm_back(
        grad_normed_two, normal_two, inverse_two, gain_two
    )
    grad_middle = upstream + grad_mid
    branch_low = grad_middle.astype(low)
    grad_mixed = contract_cols(branch_low, out_mine).astype(low)

    result = product(after(activated, grad_two), down_w)
    result = half_cols(core, middle + down_b) + (
        half_cols(core, result) + swap_core(half_cols(1 - core, result))
    )
    block_tokens, block_parts = to_tokens(result.astype(low))

    out_state = begin(mixed, branch_low)
    down_state = proceed(down_state, grad_mixed)
    grad_mixed = after(grad_mixed, *out_state[4:], down_state[2], down_state[5])
    grad_first_group = attend_back_group(stacked, grad_mixed, key_column, 0)
    down_first, down_second = finish(down_state, grad_first_group)
    down_parts = (
        jnp.concatenate([down_first, down_second], axis=1).reshape(depth, ff_rows, width).astype(low)
    )
    up_state = proceed(up_state, grad_first_group, down_parts)
    out_state = proceed(out_state, down_parts)
    down_operand = down_parts
    down_parts = trade_z(after(down_parts, block_parts))
    first_group, first_sent = scatter_start(
        *y_then_x, normed_one, after(grad_first_group, down_operand)
    )
    grad_mixed = after(
        grad_mixed, up_state[2], up_state[5], out_state[2], out_state[5], first_sent
    )
    grad_second_group = attend_back_group(stacked, grad_mixed, key_column, 1)
    second_group, second_sent = scatter_start(*x_then_y, normed_one, grad_second_group)

    def by_place(rows):
        return rows.reshape(2, depth, part_rows, -1).transpose(1, 0, 2, 3)

    def by_cols(rows):
        rows = by_place(rows).reshape(depth, 2 * part_rows, 3 * group)
        return [rows[..., k * group : (k + 1) * group] for k in range(3)]

    up_first, up_second = finish(up_state, second_sent)
    out_first, out_second = finish(out_state, second_sent)
    wide_parts = jnp.concatenate(
        [
            by_place(up_first).reshape(depth, 2 * part_rows, width),
            by_place(up_second).reshape(depth, 2 * part_rows, width),
            jnp.concatenate([out_first, out_second], axis=1).reshape(depth, part_rows, width),
        ],
        axis=1,
    ).astype(low)
    wide_operand = wide_parts
    wide_parts = trade_z(after(wide_parts, down_parts))

    first_kept, first_got, first_sent = scatter_next(
        along_y,
        here_y,
        here_x,
        swap_x,
        *lax.optimization_barrier((normed_one, grad_first_group, first_group, wide_operand))[:3],
    )

    grad_one = contract_cols(
        after(grad_second_group, first_sent), qkv_w[:, 3 * group :]
    ) + contract_cols(grad_first_group, qkv_w[:, : 3 * group])
    scaled = grad_one * gain_one
    sums = jnp.concatenate(
        [
            jnp.sum(scaled, axis=1, keepdims=True),
            jnp.sum(scaled * normal_one, axis=1, keepdims=True),
        ],
        axis=1,
    )
    got = swap_core(
        jnp.concatenate(
            [half_cols(1 - core, grad_one), jnp.pad(sums, ((0, 0), (0, 126)))], axis=1
        ),
    )

    grad_normed_one = half_cols(core, grad_one) + got[:, :half]
    means = (sums + got[:, half : half + 2]) / width
    normal_mine = half_cols(core, normal_one)
    grad_first = inverse_one * (
        grad_normed_one * half_cols(core, gain_one) - means[:, :1] - normal_mine * means[:, 1:]
    )
    input_half = (half_cols(core, grad_middle) + grad_first).astype(low)

    second_kept, second_got, _ = scatter_next(
        along_x,
        here_x,
        here_y,
        swap_y,
        *lax.optimization_barrier((normed_one, grad_second_group, second_group, grad_one))[:3],
    )
    project_first = first_kept + after(first_got, input_half)
    project_second = second_kept + after(second_got, input_half)

    first_bias = jnp.sum(grad_first_group.astype(jnp.float32), axis=0)
    second_bias = jnp.sum(grad_second_group.astype(jnp.float32), axis=0)

    def placed(mine):
        none = jnp.zeros_like(mine)
        return side_by_side(core, mine, none)

    bias_parts = jnp.stack(
        [
            jnp.concatenate([first_bias[:group], second_bias[:group]]),
            jnp.concatenate([first_bias[2 * group :], second_bias[2 * group :]]),
        ]
    ).reshape(2, planes, block)
    bias_parts = in_order(core, bias_parts, jnp.zeros_like(bias_parts), 2).reshape(2, width)
    first_core = (core == 0).astype(jnp.float32)
    small_grads = jnp.stack(
        [
            jnp.sum(grad_one * normal_one, axis=0),
            jnp.sum(grad_one, axis=0),
            bias_parts[0],
            bias_parts[1],
            first_core * jnp.sum(branch_low.astype(jnp.float32), axis=0),
            first_core * grad_gain_two,
            first_core * grad_shift_two,
            placed(jnp.sum(upstream_half.astype(jnp.float32), axis=0)),
        ]
    )
    small_wide = small_grads.reshape(count, 2 * planes * depth, part_rows)
    small_wide = small_wide.transpose(1, 0, 2).reshape(planes, 2, depth, count * part_rows)
    grad_up_b = jnp.sum(grad_hidden.astype(jnp.float32), axis=0).reshape(planes, depth, -1)
    grad_up_b = in_order(core, grad_up_b, jnp.zeros_like(grad_up_b), 1)
    small_wide = jnp.concatenate([small_wide, grad_up_b], axis=-1).reshape(2, 2, -1)
    small_sum = take(here_y, small_wide) + swap_y(take(1 - here_y, small_wide))
    small_sum = take(here_x, small_sum) + swap_x(take(1 - here_x, small_sum))
    small_sum = small_sum.reshape(2, depth, small_size).transpose(1, 0, 2)
    small_sum = small_sum.reshape(depth, 2 * small_size)
    small_sum = jnp.pad(small_sum, ((0, 0), (0, 2 * half - 2 * small_size)))
    small_sum = small_sum.reshape(depth, 2, half)

    first_cols, second_cols = (by_cols(project_first), by_cols(project_second))
    base = (tok_dev + 15) // 16 * 16
    tall = 2 * part_rows
    last_parts = jnp.concatenate(
        [jnp.pad(input_half.reshape(depth, tok_dev, half), ((0, 0), (0, base - tok_dev), (0, 0)))]
        + [
            jnp.concatenate([left, right], axis=-1).astype(low)
            for left, right in zip(first_cols, second_cols)
        ]
        + [small_sum.astype(low)],
        axis=1,
    )
    last_operand = last_parts
    last_parts = trade_z(after(last_parts, wide_parts))
    down_rows = add_up(after(down_parts, last_operand))
    wide_sum = add_up(after(wide_parts, last_operand))
    out_rows = wide_sum[4 * part_rows :]
    up_pair = jnp.concatenate(
        [wide_sum[: 2 * part_rows], wide_sum[2 * part_rows : 4 * part_rows]], axis=1
    ).reshape(2, part_rows, ff_half)
    mine, other = (take(core, up_pair), swap_core(take(1 - core, up_pair)))
    up_rows = natural_cols(
        jnp.where(core == 0, mine, other), jnp.where(core == 0, other, mine), ff_block
    )

    block_out = after(block_tokens, last_operand) * live_low
    images = last_parts[:, :tok_dev].reshape(2, slot_count, tok_dev, half)
    input_grad = side_by_side(core, take(core, images), swap_core(take(1 - core, images)))
    last_sum = jnp.sum(last_parts[:, base:].astype(jnp.float32), axis=0)
    project_pair = jnp.concatenate(
        [last_sum[k * tall : (k + 1) * tall].reshape(2, part_rows, half) for k in range(3)],
        axis=-1,
    )
    mine, other = (take(core, project_pair), swap_core(take(1 - core, project_pair)))
    small_pair = last_sum[3 * tall :].reshape(2 * half)[: 2 * small_size].reshape(2, small_size)
    small_out = take(core, small_pair) + swap_core(take(1 - core, small_pair))
    even = jnp.where(core == 0, mine, other)
    odd = jnp.where(core == 0, other, mine)

    query_rows, key_rows, value_rows = [
        natural_cols(
            even[:, k * half : (k + 1) * half], odd[:, k * half : (k + 1) * half], block
        )
        for k in range(3)
    ]
    pieces = [small_out[k * part_rows : (k + 1) * part_rows] for k in range(count)]
    return (
        block_out,
        input_grad,
        pieces[0],
        pieces[1],
        query_rows,
        pieces[2],
        key_rows,
        value_rows,
        pieces[3],
        out_rows,
        pieces[4],
        pieces[5],
        pieces[6],
        up_rows,
        small_out[count * part_rows : small_size],
        down_rows,
        pieces[7],
    )


def named_image(*args):
    return own_image(*args)


def solution(mesh):
    dp, seq = (mesh.shape["dp"], mesh.shape["seq"])
    function, axes, by_image, by_part = (per_device, mesh, "dp", ("dp", "seq"))
    by_token = "seq"
    if dp == 8 and seq == 4:
        function = named_image
        axes = jax.sharding.Mesh(mesh.devices.reshape(2, 2, 2, seq), ("y", "x", "core", "z"))
        by_image, by_token = (("y", "x", "core"), "z")
        by_part = ("y", "x", "core", "z")
    tokens, vector, matrix = (P(by_image, by_token, None), P(by_part), P(by_part, None))
    params = (
        (vector, vector, matrix, vector, matrix, matrix, vector, matrix)
        + (vector, vector, vector, matrix, vector, matrix, vector)
    )
    return jax.shard_map(
        function,
        mesh=axes,
        in_specs=(tokens, tokens, P(by_image), P(by_image, None)) + params,
        out_specs=(tokens, tokens) + params,
        check_vma=False,
    )
```
